1024 devices in a mesh: rep: 16 (over y_hi, x, core), fsdp: 64 (over y_lo, z).
Axes of the slice: x: 4, y: 8 (y_hi: 2, y_lo: 4; y = y_hi * 4 + y_lo), z: 16, core: 2. Of those that a mesh axis runs over, the one named last changes fastest.
Arguments:
- replica_grads: bfloat16 [16, 8192, 8192], P('rep', 'fsdp'), may hold values from -0.19921875 to 0.19921875
- weight: bfloat16 [8192, 8192], P('fsdp'), may hold values from -6 to 6
- moment_one: float32 [1024, 1024], P('rep', 'fsdp'), may hold values from -3 to 3
- moment_two: float32 [1024, 1024], P('rep', 'fsdp'), may hold values from 0.1 to 10
- sign_bits: int32 [8192], replicated, may hold values from 0 to 1
- kept_rows: int32 [1024], replicated, may hold values from 0 to 8191, as said below
- step_count: int32 [], replicated, may hold values from 1 to 7
Outputs:
- new_weight: bfloat16 [8192, 8192], P('fsdp')
- new_moment_one: float32 [1024, 1024], P('rep', 'fsdp')
- new_moment_two: float32 [1024, 1024], P('rep', 'fsdp')
The draws below stay inside these ranges and needn't reach their ends.
Inputs may be any that keep to these rules, and one draw needn't show every extreme that they name: `kept_rows`: all different; 0 and 8191 are always among them.
All inputs are finite; a program needn't handle non-finite values.
Results may differ from the reference program's by a relative error of at most 0.0049.
Values may be sent and summed in bfloat16 or wider, within the bound.
No kernel may reach another device: no remote copies, remote signals or barrier semaphores. Data moves between devices by JAX's collectives and lax.ppermute only.
A program may use at most 64 MiB of HBM per device.

```python
import math
import jax
import jax.numpy as jnp
from jax import lax

D = 8192
K = 1024
REPS = 16


def draw_kept_rows(key, part):
    first_key = jax.random.fold_in(key, 11)
    second_key = jax.random.fold_in(key, 23)
    others = jax.random.permutation(first_key, D - 2)[:K - 2].astype(jnp.int32) + 1
    values = jnp.concatenate([jnp.array([0, D - 1], jnp.int32), others])
    return jax.random.permutation(second_key, values)


def plant(drawn, rng, least, largest):
    dims = drawn.shape
    spot = [jax.random.randint(jax.random.fold_in(rng, axis), (), 0, dims[axis]) for axis in range(len(dims))]
    drawn = drawn.at[tuple(spot)].set(least)
    longest = dims.index(max(dims))
    spot[longest] = (spot[longest] + 1) % dims[longest]
    return drawn.at[tuple(spot)].set(largest)


def steps_of(key, shape, shards, smallest, high):
    level = 1.0
    for position, shards_of in shards:
        heights = jax.random.uniform(jax.random.fold_in(jax.random.fold_in(key, 6), position), (shards_of,), jnp.float32, smallest / len(shards), high / len(shards))
        level = level * jnp.repeat(jnp.exp(heights), shape[position] // shards_of).reshape((-1,) + (1,) * (len(shape) - 1 - position))
    return level


def gaussian(rng, extent, width, reach, pieces=(), kind=jnp.bfloat16):
    loudness = steps_of(rng, extent, pieces, -0.22, 0.18) if pieces else 1.0
    values = jax.random.normal(rng, extent, jnp.float32) * width * loudness
    return jnp.minimum(jnp.maximum(values, -reach), reach).astype(kind)


def setup_inputs(seed: int = 0) -> dict:
    splits = jax.random.split(jax.random.key(seed), 8)
    replica_grads = gaussian(splits[0], (REPS, D, D), 0.03, 0.19921875, ((0, 16), (1, 64)))
    weight = gaussian(splits[1], (D, D), 1.0, 6.0, ((0, 64),))
    moment_one = gaussian(splits[2], (K, K), 0.5, 3.0, ((0, 16), (1, 64)), jnp.float32)
    moment_two = jnp.clip(jnp.exp(math.log(10.0) - 4.6051702 * jax.random.uniform(splits[3], (K, K), jnp.float32) ** steps_of(splits[3], (K, K), ((0, 16), (1, 64)), -0.2, 0.2)), 0.1, 10.0)
    sign_bits = plant(jax.random.randint(splits[4], (D,), 0, 2), jax.random.fold_in(splits[4], 1), 0, 1).astype(jnp.int32)
    kept_rows = draw_kept_rows(jax.random.fold_in(splits[7], 71), 0)
    step_count = jax.random.randint(splits[6], (), 1, 8).astype(jnp.int32)
    return {"replica_grads": replica_grads, "weight": weight, "moment_one": moment_one, "moment_two": moment_two, "sign_bits": sign_bits, "kept_rows": kept_rows, "step_count": step_count}


BETA_ONE = 0.9
BETA_TWO = 0.95
EPSILON = 1e-08
LEARN_RATE = 0.25

def hadamard(order):
    positions = jnp.arange(order, dtype=jnp.int32)
    both = jnp.bitwise_and(positions[:, None], positions[None, :])
    parity = jnp.zeros_like(both)
    for bit_index in range(max(order.bit_length() - 1, 0)):
        parity = parity + jnp.bitwise_and(jnp.right_shift(both, bit_index), 1)
    parity = parity % 2
    return (1 - 2 * parity).astype(jnp.float32)

def transform_last(matrix):
    length = matrix.shape[-1]
    low_len = min(length, 128)
    high_len = length // low_len
    values = matrix.astype(jnp.float32).reshape(matrix.shape[:-1] + (high_len, low_len))
    values = jnp.einsum('rab,cb->rac', values, hadamard(low_len), precision=lax.Precision.HIGHEST)
    values = jnp.einsum('rab,ca->rcb', values, hadamard(high_len), precision=lax.Precision.HIGHEST)
    return values.reshape(matrix.shape)

def transform_rows(matrix):
    length = matrix.shape[0]
    low_len = min(length, 128)
    high_len = length // low_len
    values = matrix.astype(jnp.float32).reshape((high_len, low_len) + matrix.shape[1:])
    values = jnp.einsum('abc,db->adc', values, hadamard(low_len), precision=lax.Precision.HIGHEST)
    values = jnp.einsum('abc,da->dbc', values, hadamard(high_len), precision=lax.Precision.HIGHEST)
    return values.reshape(matrix.shape)

def reference(replica_grads, weight, moment_one, moment_two, sign_bits, kept_rows, step_count):
    sign_vec = (1 - 2 * sign_bits).astype(jnp.float32)
    norm_scale = 1.0 / math.sqrt(K)
    gsum = jnp.zeros((D, D), jnp.float32)
    for replica in range(REPS):
        gsum = gsum + replica_grads[replica].astype(jnp.float32)
    right_side = jnp.take(transform_last(gsum * sign_vec[None, :]), kept_rows, axis=1) * norm_scale
    compressed = jnp.take(transform_rows(right_side * sign_vec[:, None]), kept_rows, axis=0) * norm_scale
    new_one = BETA_ONE * moment_one + (1.0 - BETA_ONE) * compressed
    new_two = BETA_TWO * moment_two + (1.0 - BETA_TWO) * compressed * compressed
    steps_done = step_count.astype(jnp.float32)
    first_fix = 1.0 - jnp.power(jnp.float32(BETA_ONE), steps_done)
    second_fix = 1.0 - jnp.power(jnp.float32(BETA_TWO), steps_done)
    direction = new_one / first_fix / (jnp.sqrt(new_two / second_fix) + EPSILON)
    placed = jnp.zeros((D, K), jnp.float32).at[kept_rows].set(direction)
    back_bf = (transform_rows(placed) * sign_vec[:, None] * norm_scale).astype(jnp.bfloat16)
    col_fill = jnp.zeros((D, D), jnp.bfloat16).at[:, kept_rows].set(back_bf)
    update_full = transform_last(col_fill) * sign_vec[None, :] * norm_scale
    new_weight = (weight.astype(jnp.float32) - LEARN_RATE * update_full).astype(jnp.bfloat16)
    return (new_weight, new_one, new_two)
```

```python
import functools
import math

import jax
import jax.numpy as jnp
from jax import lax
from jax.experimental import pallas as pl
from jax.experimental.pallas import tpu as pltpu
from jax.sharding import PartitionSpec as P

BETA_ONE = 0.9
BETA_TWO = 0.95
EPSILON = 1e-08
LEARN_RATE = 0.25
LANES = 128
WIDE = 256
STEP = 1024
F32 = jnp.float32
BF16 = jnp.bfloat16


def parity_signs(left, right):
    both = jnp.bitwise_and(left, right)
    for shift in (8, 4, 2, 1):
        both = jnp.bitwise_xor(both, jnp.right_shift(both, shift))
    return (1 - 2 * jnp.bitwise_and(both, 1)).astype(F32)


def iota(shape, dim):
    return lax.broadcasted_iota(jnp.int32, shape, dim)


def wide_rows(rows, first, count):
    return jnp.concatenate([rows[first + n : first + n + 1, :] for n in range(count)], axis=1)


def column_tables_kernel(place_ref, kept_ref, one_ref, two_ref, low_ref, high_ref, send_ref, own_ref):
    half = jnp.bitwise_and(place_ref[0], 1)
    kept = kept_ref[...]
    blocks = kept.shape[0]
    digits = jnp.concatenate([jnp.right_shift(kept, 7), jnp.bitwise_and(kept, LANES - 1)], axis=0)
    digits = digits.astype(F32).astype(BF16)
    source, target = iota((LANES, LANES), 0), iota((LANES, LANES), 1)
    same = jnp.logical_and(
        jnp.right_shift(source, 4) == jnp.bitwise_and(jnp.right_shift(target, 3), 7),
        jnp.bitwise_and(source, 7) == jnp.bitwise_and(target, 7),
    )
    source_half = jnp.bitwise_and(jnp.right_shift(source, 3), 1)
    pieces = []
    for wanted in (1 - half, half):
        moved = []
        for part in (0, 1):
            pick = jnp.logical_and(same, source_half == wanted)
            pick = jnp.logical_and(pick, jnp.right_shift(target, 6) == part)
            pick = jnp.where(pick, 1.0, 0.0).astype(BF16)
            moved.append(jnp.dot(digits, pick, preferred_element_type=F32))
        for pair in range(blocks // 2):
            even, odd = 2 * pair, 2 * pair + 1
            top = moved[0][even : even + 1, :] + moved[1][odd : odd + 1, :]
            low = (
                moved[0][blocks + even : blocks + even + 1, :]
                + moved[1][blocks + odd : blocks + odd + 1, :]
            )
            pieces.append(top * LANES + low)
    columns = jnp.concatenate(pieces, axis=1).astype(jnp.int32)
    low_ref[...] = parity_signs(iota(low_ref.shape, 0), columns).astype(BF16)
    high_ref[...] = parity_signs(iota(high_ref.shape, 0), jnp.right_shift(columns, 8))
    for index, ref in enumerate((one_ref, two_ref)):
        upper, lower = ref[0:8, :], ref[8:16, :]
        blank = jnp.zeros_like(upper)
        for out, wanted in ((send_ref, 1 - half), (own_ref, half)):
            mine = jnp.where(wanted == 0, upper, lower)
            out[index] = jnp.where(
                half == 0,
                jnp.concatenate([mine, blank], axis=1),
                jnp.concatenate([blank, mine], axis=1),
            )


def row_tables_kernel(kept_ref, low_ref, high_ref):
    rows = wide_rows(kept_ref[...], 0, kept_ref.shape[0])
    low_ref[...] = parity_signs(iota(low_ref.shape, 0), rows).astype(BF16)
    high_ref[...] = parity_signs(iota(high_ref.shape, 0), jnp.right_shift(rows, 7))


def project_kernel(scale, x_ref, bits_ref, low_ref, high_ref, out_ref, acc_ref):
    step = pl.program_id(0)
    signs = (1 - 2 * bits_ref[...]).astype(F32)
    chunks = STEP // WIDE

    @pl.when(step == 0)
    def _():
        acc_ref[...] = jnp.zeros_like(acc_ref)

    total = acc_ref[...]
    for chunk in range(chunks):
        sign = wide_rows(signs, 2 * chunk, 2).astype(BF16)
        x = x_ref[:, chunk * WIDE : (chunk + 1) * WIDE] * sign
        part = jnp.dot(x, low_ref[...], preferred_element_type=F32)
        total = total + part * high_ref[pl.ds(step * chunks + chunk, 1), :]
    acc_ref[...] = total

    @pl.when(step == pl.num_programs(0) - 1)
    def _():
        done = jnp.transpose(acc_ref[...] * scale)
        out_ref[...] = done.reshape(out_ref.shape).astype(out_ref.dtype)


def compress_kernel(scale, y_ref, bits_ref, low_ref, high_ref, own_ref, got_ref, out_ref, part_ref):
    panels, width, lanes = y_ref.shape
    signs = (1 - 2 * bits_ref[...]).astype(F32)
    y = (y_ref[...].astype(F32) * signs[:, None, :]).reshape(panels * width, lanes).astype(BF16)
    part = jnp.dot(y, low_ref[...], preferred_element_type=F32)
    part_ref[...] = part.reshape(part_ref.shape)

    def add(panel, total):
        return total + part_ref[panel] * high_ref[pl.ds(panel, 1), :]

    total = lax.fori_loop(0, panels, add, jnp.zeros(part_ref.shape[1:], F32), unroll=8)
    total = (total * scale).astype(BF16)
    count = total.shape[1] // LANES
    pieces = [total[:, n * LANES : (n + 1) * LANES] for n in range(count)]
    for index in range(2):
        rest = own_ref[index] + got_ref[index]
        for _ in range(3):
            piece = rest.astype(BF16)
            pieces.append(piece)
            rest = rest - piece.astype(F32)
    for peer in range(out_ref.shape[0]):
        for n, piece in enumerate(pieces):
            out_ref[peer, n] = piece


def adam_kernel(
    scale, place_ref, fix_ref, got_ref, bits_ref, low_ref, high_ref, back_ref, sum_ref, lhs_ref
):
    peers = got_ref.shape[0]
    mine = jnp.right_shift(place_ref[0], 1)
    first_fix, second_fix = fix_ref[0], fix_ref[1]
    tops, rests = [], []
    for n in range(peers):
        total = got_ref[0, n].astype(F32)
        for peer in range(1, peers):
            total = total + got_ref[peer, n].astype(F32)

        @pl.when(mine == n)
        def _():
            sum_ref[...] = total

        one = got_ref[n, peers].astype(F32) + got_ref[n, peers + 1].astype(F32)
        one = one + got_ref[n, peers + 2].astype(F32)
        two = got_ref[n, peers + 3].astype(F32) + got_ref[n, peers + 4].astype(F32)
        two = two + got_ref[n, peers + 5].astype(F32)
        new_one = BETA_ONE * one + (1.0 - BETA_ONE) * total
        new_two = BETA_TWO * two + (1.0 - BETA_TWO) * total * total
        direction = new_one / first_fix / (jnp.sqrt(new_two / second_fix) + EPSILON)
        top = direction.astype(BF16).astype(F32)
        tops.append(top)
        rests.append(direction - top)
    both = jnp.concatenate([jnp.concatenate(tops, axis=1), jnp.concatenate(rests, axis=1)], axis=0)
    panels = lhs_ref.shape[0]

    def fill(panel, carry):
        lhs_ref[panel] = (both * high_ref[pl.ds(panel, 1), :]).astype(BF16)
        return carry

    lax.fori_loop(0, panels, fill, 0, unroll=8)
    lhs = lhs_ref[...].reshape(panels * lhs_ref.shape[1], lhs_ref.shape[2])
    back = lax.dot_general(lhs, low_ref[...], (((1,), (1,)), ((), ())), preferred_element_type=F32)
    back = back.reshape(panels, 2, back.shape[0] // panels // 2, LANES)
    signs = (1 - 2 * bits_ref[...]).astype(F32) * scale
    back_ref[...] = ((back[:, 0] + back[:, 1]) * signs[:, None, :]).astype(BF16)


def expand_kernel(scale, other_ref, own_ref, low_ref, high_ref, bits_ref, weight_ref, out_ref,
                  back_ref, table_ref, lhs_ref):
    step = pl.program_id(0)
    rows = weight_ref.shape[0]
    chunks = STEP // WIDE

    @pl.when(step == 0)
    def _():
        for index, ref in enumerate((other_ref, own_ref)):
            half = ref.shape[0] * ref.shape[1]
            columns = ref[...].astype(F32).reshape(half, rows)
            back_ref[:, index * half : (index + 1) * half] = jnp.transpose(columns)
        table_ref[...] = jnp.transpose(low_ref[...].astype(F32)).astype(BF16)

    for chunk in range(chunks):
        sign = high_ref[pl.ds(step * chunks + chunk, 1), :]
        lhs_ref[chunk * rows : (chunk + 1) * rows, :] = (back_ref[...] * sign).astype(BF16)
    update = jnp.dot(lhs_ref[...], table_ref[...], preferred_element_type=F32)
    signs = (1 - 2 * bits_ref[...]).astype(F32) * scale
    for chunk in range(chunks):
        lanes = slice(chunk * WIDE, (chunk + 1) * WIDE)
        moved = update[chunk * rows : (chunk + 1) * rows, :] * wide_rows(signs, 2 * chunk, 2)
        out_ref[:, lanes] = (weight_ref[:, lanes].astype(F32) - moved).astype(BF16)


def shaped(shape, dtype):
    return jax.ShapeDtypeStruct(shape, dtype)


SMEM = pl.BlockSpec(memory_space=pltpu.SMEM)
VMEM = pl.BlockSpec(memory_space=pltpu.VMEM)


def cost(flops, moved):
    return pl.CostEstimate(flops=flops, bytes_accessed=moved, transcendentals=0)


def local(replica_grads, weight, moment_one, moment_two, sign_bits, kept_rows, step_count):
    reps, panels = lax.axis_size("rep"), lax.axis_size("fsdp")
    full_len, kept_len = sign_bits.shape[0], kept_rows.shape[0]
    rows = weight.shape[0]
    peers = reps // 2
    half_width = kept_len // panels // 2
    half_len = kept_len // 2
    norm_scale = 1.0 / math.sqrt(kept_len)
    place = lax.axis_index("rep").astype(jnp.int32).reshape(1)
    half = jnp.bitwise_and(place[0], 1)
    kept = kept_rows.reshape(kept_len // LANES, LANES)
    bits = sign_bits.reshape(full_len // LANES, LANES)
    one_t, two_t = moment_one.T, moment_two.T
    swap = [(n, n ^ 1) for n in range(reps)]
    wide_count = full_len // WIDE

    col_low, col_high, send_moments, own_moments = pl.pallas_call(
        column_tables_kernel,
        out_shape=(
            shaped((WIDE, kept_len), BF16),
            shaped((wide_count, kept_len), F32),
            shaped((2, half_width, LANES), F32),
            shaped((2, half_width, LANES), F32),
        ),
        in_specs=[SMEM, VMEM, VMEM, VMEM],
        out_specs=(VMEM,) * 4,
        cost_estimate=cost(10 * WIDE * kept_len, 2 * WIDE * kept_len),
    )(place, kept, one_t, two_t)

    def project(index, dtype):
        shape = (panels, half_width, rows)
        return pl.pallas_call(
            functools.partial(project_kernel, norm_scale),
            grid=(full_len // STEP,),
            out_shape=shaped(shape, dtype),
            in_specs=[
                pl.BlockSpec((None, rows, STEP), lambda i: (0, 0, i)),
                pl.BlockSpec((STEP // LANES, LANES), lambda i: (i, 0)),
                pl.BlockSpec((WIDE, half_len), lambda i: (0, index)),
                pl.BlockSpec((wide_count, half_len), lambda i: (0, index)),
            ],
            out_specs=pl.BlockSpec(shape, lambda i: (0, 0, 0)),
            scratch_shapes=[pltpu.VMEM((rows, half_len), F32)],
            cost_estimate=cost(2 * rows * full_len * half_len, 2 * rows * full_len),
        )(replica_grads, bits, col_low, col_high)

    for_other = project(0, BF16)
    from_other = lax.ppermute(for_other, "rep", swap)
    got_moments = lax.ppermute(send_moments, "rep", swap)
    mine = project(1, F32)
    row_low, row_high = pl.pallas_call(
        row_tables_kernel,
        out_shape=(shaped((LANES, kept_len), BF16), shaped((panels, kept_len), F32)),
        in_specs=[VMEM],
        out_specs=(VMEM,) * 2,
        cost_estimate=cost(10 * LANES * kept_len, 2 * LANES * kept_len),
    )(kept)
    columns = (mine + from_other.astype(F32)).astype(BF16)
    columns = lax.all_to_all(columns, "fsdp", 0, 0)

    message = pl.pallas_call(
        functools.partial(compress_kernel, norm_scale),
        out_shape=shaped((peers, kept_len // LANES + 6, half_width, LANES), BF16),
        in_specs=[VMEM] * 6,
        out_specs=VMEM,
        scratch_shapes=[pltpu.VMEM((panels, half_width, kept_len), F32)],
        cost_estimate=cost(2 * full_len * half_width * kept_len // panels, 2 * full_len * half_width),
    )(columns, bits, row_low, row_high, own_moments, got_moments)
    groups = [list(range(core, reps, 2)) for core in (0, 1)]
    message = lax.all_to_all(message, "rep", 0, 0, axis_index_groups=groups)

    steps_done = step_count.astype(F32)
    fixes = jnp.stack(
        [1.0 - jnp.power(F32(BETA_ONE), steps_done), 1.0 - jnp.power(F32(BETA_TWO), steps_done)]
    )
    back, own_sum = pl.pallas_call(
        functools.partial(adam_kernel, norm_scale),
        out_shape=(
            shaped((panels, half_width, rows), BF16),
            shaped((half_width, LANES), F32),
        ),
        in_specs=[SMEM, SMEM] + [VMEM] * 4,
        out_specs=(VMEM,) * 2,
        scratch_shapes=[pltpu.VMEM((panels, 2 * half_width, kept_len), BF16)],
        cost_estimate=cost(4 * full_len * half_width * kept_len, 2 * full_len * half_width),
    )(place, fixes, message, bits, row_low, row_high)
    other_sum = lax.ppermute(own_sum, "rep", swap)
    back = lax.all_to_all(back, "fsdp", 0, 0)
    other_back = lax.ppermute(back, "rep", swap)

    row_count = moment_one.shape[0]
    own_rows = jnp.where(half == 0, own_sum[:, :row_count], own_sum[:, row_count:])
    other_rows = jnp.where(half == 0, other_sum[:, :row_count], other_sum[:, row_count:])
    compressed = jnp.where(
        half == 0,
        jnp.concatenate([own_rows, other_rows], axis=0),
        jnp.concatenate([other_rows, own_rows], axis=0),
    )
    new_one = (BETA_ONE * one_t + (1.0 - BETA_ONE) * compressed).T
    new_two = (BETA_TWO * two_t + (1.0 - BETA_TWO) * compressed * compressed).T

    back_shape = (panels, half_width, rows)
    new_weight = pl.pallas_call(
        functools.partial(expand_kernel, LEARN_RATE * norm_scale),
        grid=(full_len // STEP,),
        out_shape=shaped(weight.shape, BF16),
        in_specs=[
            pl.BlockSpec(back_shape, lambda i: (0, 0, 0)),
            pl.BlockSpec(back_shape, lambda i: (0, 0, 0)),
            pl.BlockSpec((WIDE, kept_len), lambda i: (0, 0)),
            pl.BlockSpec((wide_count, kept_len), lambda i: (0, 0)),
            pl.BlockSpec((STEP // LANES, LANES), lambda i: (i, 0)),
            pl.BlockSpec((rows, STEP), lambda i: (0, i)),
        ],
        out_specs=pl.BlockSpec((rows, STEP), lambda i: (0, i)),
        scratch_shapes=[
            pltpu.VMEM((rows, kept_len), F32),
            pltpu.VMEM((kept_len, WIDE), BF16),
            pltpu.VMEM((rows * STEP // WIDE, kept_len), BF16),
        ],
        cost_estimate=cost(2 * rows * full_len * kept_len, 4 * rows * full_len),
    )(other_back, back, col_low, col_high, bits, weight)
    return (new_weight, new_one, new_two)


def solution(mesh):
    in_specs = (
        P("rep", "fsdp", None),
        P("fsdp", None),
        P("rep", "fsdp"),
        P("rep", "fsdp"),
        P(),
        P(),
        P(),
    )
    out_specs = (P("fsdp", None), P("rep", "fsdp"), P("rep", "fsdp"))
    return jax.shard_map(local, mesh=mesh, in_specs=in_specs, out_specs=out_specs, check_vma=False)
```

```python
import functools
import math

import jax
import jax.numpy as jnp
from jax import lax
from jax.experimental import pallas as pl
from jax.experimental.pallas import tpu as pltpu
from jax.sharding import PartitionSpec as P

BETA_ONE = 0.9
BETA_TWO = 0.95
EPSILON = 1e-08
LEARN_RATE = 0.25
LANES = 128
WIDE = 256
STEP = 1024
LONG_STEP = 2048
F32 = jnp.float32
BF16 = jnp.bfloat16


def parity_signs(left, right):
    both = jnp.bitwise_and(left, right)
    for shift in (4, 2, 1):
        both = jnp.bitwise_xor(both, jnp.right_shift(both, shift))
    return (1 - 2 * jnp.bitwise_and(both, 1)).astype(F32)


def iota(shape, dim):
    return lax.broadcasted_iota(jnp.int32, shape, dim)


def wide_rows(rows, first, count):
    return jnp.concatenate([rows[first + n : first + n + 1, :] for n in range(count)], axis=1)


def fill_low_table(ref, columns):
    count = 16
    shape = (count, columns.shape[1])
    fine = parity_signs(iota(shape, 0), columns)
    coarse = parity_signs(iota(shape, 0), jnp.right_shift(columns, 4))
    for n in range(ref.shape[0] // count):
        ref[n * count : (n + 1) * count, :] = (fine * coarse[n : n + 1, :]).astype(BF16)


def order_columns(half, kept):
    blocks = kept.shape[0]
    digits = jnp.concatenate([jnp.right_shift(kept, 7), jnp.bitwise_and(kept, LANES - 1)], axis=0)
    digits = digits.astype(F32).astype(BF16)
    source, target = iota((LANES, LANES), 0), iota((LANES, LANES), 1)
    same = jnp.logical_and(
        jnp.right_shift(source, 4) == jnp.bitwise_and(jnp.right_shift(target, 3), 7),
        jnp.bitwise_and(source, 7) == jnp.bitwise_and(target, 7),
    )
    source_half = jnp.bitwise_and(jnp.right_shift(source, 3), 1)
    pieces = []
    for wanted in (1 - half, half):
        moved = []
        for part in (0, 1):
            pick = jnp.logical_and(same, source_half == wanted)
            pick = jnp.logical_and(pick, jnp.right_shift(target, 6) == part)
            pick = jnp.where(pick, 1.0, 0.0).astype(BF16)
            moved.append(jnp.dot(digits, pick, preferred_element_type=F32))
        for pair in range(blocks // 2):
            even, odd = 2 * pair, 2 * pair + 1
            top = moved[0][even : even + 1, :] + moved[1][odd : odd + 1, :]
            low = (
                moved[0][blocks + even : blocks + even + 1, :]
                + moved[1][blocks + odd : blocks + odd + 1, :]
            )
            pieces.append(top * LANES + low)
    return jnp.concatenate(pieces, axis=1).astype(jnp.int32)


def project_half(scale, first, x_of, low_ref, high_ref, out_ref, acc_ref):
    rows, width = acc_ref.shape
    chunks = STEP // WIDE
    columns = slice(first, first + width)
    acc_ref[...] = jnp.zeros_like(acc_ref)

    def add(step, carry):
        x = x_of(step)
        stacked = jnp.concatenate([x[:, n * WIDE : (n + 1) * WIDE] for n in range(chunks)], axis=0)
        part = jnp.dot(stacked, low_ref[:, columns], preferred_element_type=F32)
        total = acc_ref[...]
        for n in range(chunks):
            sign = high_ref[pl.ds(step * chunks + n, 1), columns]
            total = total + part[n * rows : (n + 1) * rows, :] * sign
        acc_ref[...] = total
        return carry

    steps = high_ref.shape[0] // chunks
    lax.fori_loop(0, steps, add, 0)
    done = jnp.transpose(acc_ref[...] * scale)
    out_ref[...] = done.reshape(out_ref.shape).astype(out_ref.dtype)


def project_other_kernel(
    scale, place_ref, kept_ref, one_ref, two_ref, bits_ref, x_ref,
    low_ref, high_ref, send_ref, own_ref, signed_ref, out_ref, acc_ref, sems
):
    def fetch(step):
        lanes = pl.ds(pl.multiple_of(step * STEP, STEP), STEP)
        return pltpu.make_async_copy(x_ref.at[0, :, lanes], signed_ref.at[:, lanes], sems.at[step])

    for step in range(signed_ref.shape[1] // STEP):
        fetch(step).start()
    half = jnp.bitwise_and(place_ref[0], 1)
    columns = order_columns(half, kept_ref[...])
    fill_low_table(low_ref, columns)
    high_ref[...] = parity_signs(iota(high_ref.shape, 0), jnp.right_shift(columns, 8))
    for index, ref in enumerate((one_ref, two_ref)):
        upper, lower = ref[0:8, :], ref[8:16, :]
        blank = jnp.zeros_like(upper)
        for out, wanted in ((send_ref, 1 - half), (own_ref, half)):
            mine = jnp.where(wanted == 0, upper, lower)
            out[index] = jnp.where(
                half == 0,
                jnp.concatenate([mine, blank], axis=1),
                jnp.concatenate([blank, mine], axis=1),
            )

    def x_of(step):
        fetch(step).wait()
        lanes = pl.ds(pl.multiple_of(step * STEP, STEP), STEP)
        signs = (1 - 2 * bits_ref[pl.ds(step * (STEP // LANES), STEP // LANES), :]).astype(F32)
        x = signed_ref[:, lanes] * wide_rows(signs, 0, STEP // LANES).astype(BF16)
        signed_ref[:, lanes] = x
        return x

    project_half(scale, 0, x_of, low_ref, high_ref, out_ref, acc_ref)


def project_own_kernel(scale, signed_ref, low_ref, high_ref, out_ref, acc_ref):
    def x_of(step):
        return signed_ref[:, pl.ds(pl.multiple_of(step * STEP, STEP), STEP)]

    project_half(scale, acc_ref.shape[1], x_of, low_ref, high_ref, out_ref, acc_ref)


def row_tables_kernel(kept_ref, low_ref, high_ref):
    rows = wide_rows(kept_ref[...], 0, kept_ref.shape[0])
    fill_low_table(low_ref, rows)
    high_ref[...] = parity_signs(iota(high_ref.shape, 0), jnp.right_shift(rows, 8))


def row_turned_kernel(kept_ref, when_ref, turned_ref, high_ref, low_ref):
    row_tables_kernel(kept_ref, low_ref, high_ref)
    turned_ref[...] = jnp.transpose(low_ref[...].astype(F32)).astype(BF16)


def column_turned_kernel(place_ref, kept_ref, when_ref, turned_ref, high_ref, low_ref):
    columns = order_columns(jnp.bitwise_and(place_ref[0], 1), kept_ref[...])
    fill_low_table(low_ref, columns)
    high_ref[...] = parity_signs(iota(high_ref.shape, 0), jnp.right_shift(columns, 8))
    turned_ref[...] = jnp.transpose(low_ref[...].astype(F32)).astype(BF16)


def compress_kernel(scale, y_ref, bits_ref, low_ref, high_ref, own_ref, got_ref, out_ref, part_ref):
    panels, width, lanes = y_ref.shape
    signs = (1 - 2 * bits_ref[...]).astype(F32)
    y = (y_ref[...].astype(F32) * signs[:, None, :]).reshape(panels // 2, 2, width, lanes)
    y = jnp.concatenate([y[:, 0], y[:, 1]], axis=2).reshape(panels // 2 * width, 2 * lanes)
    part = jnp.dot(y.astype(BF16), low_ref[...], preferred_element_type=F32)
    part_ref[...] = part.reshape(part_ref.shape)

    def add(panel, total):
        return total + part_ref[panel] * high_ref[pl.ds(panel, 1), :]

    total = lax.fori_loop(0, panels // 2, add, jnp.zeros(part_ref.shape[1:], F32), unroll=8)
    total = (total * scale).astype(BF16)
    count = total.shape[1] // LANES
    pieces = [total[:, n * LANES : (n + 1) * LANES] for n in range(count)]
    for index in range(2):
        rest = own_ref[index] + got_ref[index]
        for _ in range(3):
            piece = rest.astype(BF16)
            pieces.append(piece)
            rest = rest - piece.astype(F32)
    for peer in range(out_ref.shape[0]):
        for n, piece in enumerate(pieces):
            out_ref[peer, n] = piece


def adam_kernel(
    scale, place_ref, fix_ref, got_ref, bits_ref, turned_ref, high_ref, back_ref, sum_ref, lhs_ref
):
    peers = got_ref.shape[0]
    mine = jnp.right_shift(place_ref[0], 1)
    first_fix, second_fix = fix_ref[0], fix_ref[1]
    tops, rests = [], []
    own = jnp.zeros(sum_ref.shape, F32)
    for n in range(peers):
        total = got_ref[0, n].astype(F32)
        for peer in range(1, peers):
            total = total + got_ref[peer, n].astype(F32)
        own = jnp.where(mine == n, total, own)
        one = got_ref[n, peers].astype(F32) + got_ref[n, peers + 1].astype(F32)
        one = one + got_ref[n, peers + 2].astype(F32)
        two = got_ref[n, peers + 3].astype(F32) + got_ref[n, peers + 4].astype(F32)
        two = two + got_ref[n, peers + 5].astype(F32)
        new_one = BETA_ONE * one + (1.0 - BETA_ONE) * total
        new_two = BETA_TWO * two + (1.0 - BETA_TWO) * total * total
        direction = new_one / first_fix / (jnp.sqrt(new_two / second_fix) + EPSILON)
        top = direction.astype(BF16).astype(F32)
        tops.append(top)
        rests.append(direction - top)
    sum_ref[...] = own
    both = jnp.concatenate([jnp.concatenate(tops, axis=1), jnp.concatenate(rests, axis=1)], axis=0)
    wides = lhs_ref.shape[0]

    def fill(wide, carry):
        lhs_ref[wide] = (both * high_ref[pl.ds(wide, 1), :]).astype(BF16)
        return carry

    lax.fori_loop(0, wides, fill, 0, unroll=8)
    lhs = lhs_ref[...].reshape(wides * lhs_ref.shape[1], lhs_ref.shape[2])
    back = jnp.dot(lhs, turned_ref[...], preferred_element_type=F32)
    back = back.reshape(wides, 2, back.shape[0] // wides // 2, WIDE)
    back = back[:, 0] + back[:, 1]
    back = jnp.stack([back[:, :, :LANES], back[:, :, LANES:]], axis=1).reshape(back_ref.shape)
    signs = (1 - 2 * bits_ref[...]).astype(F32) * scale
    back_ref[...] = (back * signs[:, None, :]).astype(BF16)


def expand_kernel(scale, other_ref, own_ref, turned_ref, high_ref, bits_ref, weight_ref, out_ref,
                  back_ref, lhs_ref):
    step = pl.program_id(0)
    rows = weight_ref.shape[0]
    stride = out_ref.shape[1]
    chunks = stride // WIDE

    @pl.when(step == 0)
    def _():
        for index, ref in enumerate((other_ref, own_ref)):
            half = ref.shape[0] * ref.shape[1]
            columns = ref[...].astype(F32).reshape(half, rows)
            back_ref[:, index * half : (index + 1) * half] = jnp.transpose(columns).astype(BF16)

    for chunk in range(chunks):
        sign = high_ref[pl.ds(step * chunks + chunk, 1), :].astype(BF16)
        lhs_ref[chunk * rows : (chunk + 1) * rows, :] = back_ref[...] * sign
    update = jnp.dot(lhs_ref[...], turned_ref[...], preferred_element_type=F32)
    tiles = stride // LANES
    signs = (1 - 2 * bits_ref[pl.ds(step * tiles, tiles), :]).astype(F32) * scale
    for chunk in range(chunks):
        lanes = pl.ds(pl.multiple_of(step * stride + chunk * WIDE, WIDE), WIDE)
        moved = update[chunk * rows : (chunk + 1) * rows, :] * wide_rows(signs, 2 * chunk, 2)
        moved = weight_ref[:, lanes].astype(F32) - moved
        out_ref[:, chunk * WIDE : (chunk + 1) * WIDE] = moved.astype(BF16)


def shaped(shape, dtype):
    return jax.ShapeDtypeStruct(shape, dtype)


SMEM = pl.BlockSpec(memory_space=pltpu.SMEM)
ROOM = pltpu.CompilerParams(vmem_limit_bytes=24 << 20)
VMEM = pl.BlockSpec(memory_space=pltpu.VMEM)


def cost(flops, moved):
    return pl.CostEstimate(flops=flops, bytes_accessed=moved, transcendentals=0)


def local(replica_grads, weight, moment_one, moment_two, sign_bits, kept_rows, step_count):
    reps, panels = lax.axis_size("rep"), lax.axis_size("fsdp")
    full_len, kept_len = sign_bits.shape[0], kept_rows.shape[0]
    rows = weight.shape[0]
    peers = reps // 2
    half_width = kept_len // panels // 2
    half_len = kept_len // 2
    norm_scale = 1.0 / math.sqrt(kept_len)
    place = lax.axis_index("rep").astype(jnp.int32).reshape(1)
    half = jnp.bitwise_and(place[0], 1)
    kept = kept_rows.reshape(kept_len // LANES, LANES)
    bits = sign_bits.reshape(full_len // LANES, LANES)
    one_t, two_t = moment_one.T, moment_two.T
    swap = [(n, n ^ 1) for n in range(reps)]
    wide_count = full_len // WIDE

    half_shape = (panels, half_width, rows)
    col_low, col_high, send_moments, own_moments, signed, for_other = pl.pallas_call(
        functools.partial(project_other_kernel, norm_scale),
        out_shape=(
            shaped((WIDE, kept_len), BF16),
            shaped((wide_count, kept_len), F32),
            shaped((2, half_width, LANES), F32),
            shaped((2, half_width, LANES), F32),
            shaped((rows, full_len), BF16),
            shaped(half_shape, BF16),
        ),
        in_specs=[SMEM] + [VMEM] * 4 + [pl.BlockSpec(memory_space=pltpu.HBM)],
        out_specs=(VMEM,) * 6,
        scratch_shapes=[
            pltpu.VMEM((rows, half_len), F32),
            pltpu.SemaphoreType.DMA((full_len // STEP,)),
        ],
        compiler_params=ROOM,
        cost_estimate=cost(2 * rows * full_len * half_len, 2 * rows * full_len),
    )(place, kept, one_t, two_t, bits, pltpu.with_memory_space_constraint(replica_grads, pltpu.HBM))
    from_other = lax.ppermute(for_other, "rep", swap)
    mine = pl.pallas_call(
        functools.partial(project_own_kernel, norm_scale),
        out_shape=shaped(half_shape, F32),
        in_specs=[VMEM] * 3,
        out_specs=VMEM,
        scratch_shapes=[pltpu.VMEM((rows, half_len), F32)],
        compiler_params=ROOM,
        cost_estimate=cost(2 * rows * full_len * half_len, 2 * rows * full_len),
    )(signed, col_low, col_high)
    got_moments = lax.ppermute(send_moments, "rep", swap)
    row_low, row_high = pl.pallas_call(
        row_tables_kernel,
        out_shape=(shaped((WIDE, kept_len), BF16), shaped((wide_count, kept_len), F32)),
        in_specs=[VMEM],
        out_specs=(VMEM,) * 2,
        compiler_params=ROOM,
        cost_estimate=cost(10 * LANES * kept_len, 8 * WIDE * kept_len),
    )(kept)

    def turned(kernel, smem, *operands):
        return pl.pallas_call(
            kernel,
            out_shape=(shaped((kept_len, WIDE), BF16), shaped((wide_count, kept_len), F32)),
            in_specs=[SMEM] * smem + [VMEM, pl.BlockSpec(memory_space=pl.ANY)],
            out_specs=(VMEM,) * 2,
            scratch_shapes=[pltpu.VMEM((WIDE, kept_len), BF16)],
            compiler_params=ROOM,
            cost_estimate=cost(10 * LANES * kept_len, 8 * WIDE * kept_len),
        )(*operands)

    columns = (mine + from_other.astype(F32)).astype(BF16)
    columns = lax.all_to_all(columns, "fsdp", 0, 0)

    message = pl.pallas_call(
        functools.partial(compress_kernel, norm_scale),
        out_shape=shaped((peers, kept_len // LANES + 6, half_width, LANES), BF16),
        in_specs=[VMEM] * 6,
        out_specs=VMEM,
        scratch_shapes=[pltpu.VMEM((panels // 2, half_width, kept_len), F32)],
        compiler_params=ROOM,
        cost_estimate=cost(2 * full_len * half_width * kept_len // panels, 2 * full_len * half_width),
    )(columns, bits, row_low, row_high, own_moments, got_moments)
    row_turned, row_high = turned(row_turned_kernel, 0, kept, message)
    groups = [list(range(core, reps, 2)) for core in (0, 1)]
    message = lax.all_to_all(message, "rep", 0, 0, axis_index_groups=groups)

    steps_done = step_count.astype(F32)
    fixes = jnp.stack(
        [1.0 - jnp.power(F32(BETA_ONE), steps_done), 1.0 - jnp.power(F32(BETA_TWO), steps_done)]
    )
    back, own_sum = pl.pallas_call(
        functools.partial(adam_kernel, norm_scale),
        out_shape=(
            shaped((panels, half_width, rows), BF16),
            shaped((half_width, LANES), F32),
        ),
        in_specs=[SMEM, SMEM] + [VMEM] * 4,
        out_specs=(VMEM,) * 2,
        scratch_shapes=[pltpu.VMEM((wide_count, 2 * half_width, kept_len), BF16)],
        compiler_params=ROOM,
        cost_estimate=cost(4 * full_len * half_width * kept_len, 2 * full_len * half_width),
    )(place, fixes, message, bits, row_turned, row_high)
    col_turned, col_high = turned(column_turned_kernel, 1, place, kept, back)
    other_sum = lax.ppermute(own_sum, "rep", swap)
    back = lax.all_to_all(back, "fsdp", 0, 0)
    other_back = lax.ppermute(back, "rep", swap)

    row_count = moment_one.shape[0]
    own_rows = jnp.where(half == 0, own_sum[:, :row_count], own_sum[:, row_count:])
    other_rows = jnp.where(half == 0, other_sum[:, :row_count], other_sum[:, row_count:])
    compressed = jnp.where(
        half == 0,
        jnp.concatenate([own_rows, other_rows], axis=0),
        jnp.concatenate([other_rows, own_rows], axis=0),
    )
    new_one = (BETA_ONE * one_t + (1.0 - BETA_ONE) * compressed).T
    new_two = (BETA_TWO * two_t + (1.0 - BETA_TWO) * compressed * compressed).T

    new_weight = pl.pallas_call(
        functools.partial(expand_kernel, LEARN_RATE * norm_scale),
        grid=(full_len // LONG_STEP,),
        out_shape=shaped(weight.shape, BF16),
        in_specs=[VMEM] * 6,
        out_specs=pl.BlockSpec((rows, LONG_STEP), lambda i: (0, i)),
        scratch_shapes=[
            pltpu.VMEM((rows, kept_len), BF16),
            pltpu.VMEM((rows * LONG_STEP // WIDE, kept_len), BF16),
        ],
        compiler_params=ROOM,
        cost_estimate=cost(2 * rows * full_len * kept_len, 4 * rows * full_len),
    )(other_back, back, col_turned, col_high, bits, weight)
    return (new_weight, new_one, new_two)


def solution(mesh):
    in_specs = (
        P("rep", "fsdp", None),
        P("fsdp", None),
        P("rep", "fsdp"),
        P("rep", "fsdp"),
        P(),
        P(),
        P(),
    )
    out_specs = (P("fsdp", None), P("rep", "fsdp"), P("rep", "fsdp"))
    return jax.shard_map(local, mesh=mesh, in_specs=in_specs, out_specs=out_specs, check_vma=False)
```

```python
import functools
import math

import jax
import jax.numpy as jnp
from jax import lax
from jax.experimental import pallas as pl
from jax.experimental.pallas import tpu as pltpu
from jax.sharding import PartitionSpec as P

BETA_ONE = 0.9
BETA_TWO = 0.95
EPSILON = 1e-08
LEARN_RATE = 0.25
LANES = 128
WIDE = 256
STEP = 1024
LONG_STEP = 2048
F32 = jnp.float32
BF16 = jnp.bfloat16


def parity_signs(left, right):
    both = jnp.bitwise_and(left, right)
    for shift in (4, 2, 1):
        both = jnp.bitwise_xor(both, jnp.right_shift(both, shift))
    return (1 - 2 * jnp.bitwise_and(both, 1)).astype(F32)


def iota(shape, dim):
    return lax.broadcasted_iota(jnp.int32, shape, dim)


def wide_rows(rows, first, count):
    return jnp.concatenate([rows[first + n : first + n + 1, :] for n in range(count)], axis=1)


def fill_low_table(ref, columns):
    count = 16
    shape = (count, columns.shape[1])
    fine = parity_signs(iota(shape, 0), columns)
    coarse = parity_signs(iota(shape, 0), jnp.right_shift(columns, 4))
    for n in range(ref.shape[0] // count):
        ref[n * count : (n + 1) * count, :] = (fine * coarse[n : n + 1, :]).astype(BF16)


def fill_tables(kept, low_ref, high_ref):
    rows = wide_rows(kept, 0, kept.shape[0])
    fill_low_table(low_ref, rows)
    high_ref[...] = parity_signs(iota(high_ref.shape, 0), jnp.right_shift(rows, 8))


def project_kernel(scale, kept_ref, bits_ref, x_ref, out_ref, low_ref, high_ref, raw_ref, acc_ref, sems):
    rows, width = acc_ref.shape
    chunks = STEP // WIDE
    tiles = STEP // LANES

    def fetch(step):
        lanes = pl.ds(pl.multiple_of(step * STEP, STEP), STEP)
        return pltpu.make_async_copy(x_ref.at[0, :, lanes], raw_ref.at[:, lanes], sems.at[step])

    steps = raw_ref.shape[1] // STEP
    for step in range(steps):
        fetch(step).start()
    fill_tables(kept_ref[...], low_ref, high_ref)
    acc_ref[...] = jnp.zeros_like(acc_ref)

    def add(step, carry):
        fetch(step).wait()
        signs = (1 - 2 * bits_ref[pl.ds(step * tiles, tiles), :]).astype(F32)
        pieces = []
        for n in range(chunks):
            lanes = pl.ds(pl.multiple_of(step * STEP + n * WIDE, WIDE), WIDE)
            pieces.append(raw_ref[:, lanes] * wide_rows(signs, 2 * n, 2).astype(BF16))
        stacked = jnp.concatenate(pieces, axis=0)
        for first in range(0, width, WIDE):
            columns = slice(first, first + WIDE)
            part = jnp.dot(stacked, low_ref[:, columns], preferred_element_type=F32)
            total = acc_ref[:, columns]
            for n in range(chunks):
                sign = high_ref[pl.ds(step * chunks + n, 1), columns]
                total = total + part[n * rows : (n + 1) * rows, :] * sign
            acc_ref[:, columns] = total
        return carry

    lax.fori_loop(0, steps, add, 0)
    done = jnp.transpose(acc_ref[...] * scale)
    out_ref[...] = done.reshape(out_ref.shape).astype(out_ref.dtype)


def tables_kernel(place_ref, kept_ref, one_ref, two_ref, when_ref, low_ref, high_ref, send_ref, own_ref):
    fill_tables(kept_ref[...], low_ref, high_ref)
    half = jnp.bitwise_and(place_ref[0], 1)
    for index, ref in enumerate((one_ref, two_ref)):
        upper, lower = ref[0:8, :], ref[8:16, :]
        blank = jnp.zeros_like(upper)
        for out, wanted in ((send_ref, 1 - half), (own_ref, half)):
            mine = jnp.where(wanted == 0, upper, lower)
            out[index] = jnp.where(
                half == 0,
                jnp.concatenate([mine, blank], axis=1),
                jnp.concatenate([blank, mine], axis=1),
            )


def turned_kernel(kept_ref, when_ref, turned_ref, high_ref, low_ref):
    fill_tables(kept_ref[...], low_ref, high_ref)
    turned_ref[...] = jnp.transpose(low_ref[...].astype(F32)).astype(BF16)


def compress_kernel(scale, y_ref, bits_ref, low_ref, high_ref, own_ref, got_ref, out_ref, part_ref):
    panels, lanes = bits_ref.shape
    width = y_ref.shape[0] * y_ref.shape[1] // panels
    signs = (1 - 2 * bits_ref[...]).astype(F32)
    y = y_ref[...].astype(F32).reshape(panels, width, lanes) * signs[:, None, :]
    y = y.reshape(panels // 2, 2, width, lanes)
    y = jnp.concatenate([y[:, 0], y[:, 1]], axis=2).reshape(panels // 2 * width, 2 * lanes)
    part = jnp.dot(y.astype(BF16), low_ref[...], preferred_element_type=F32)
    part_ref[...] = part.reshape(part_ref.shape)

    def add(panel, total):
        return total + part_ref[panel] * high_ref[pl.ds(panel, 1), :]

    total = lax.fori_loop(0, panels // 2, add, jnp.zeros(part_ref.shape[1:], F32), unroll=8)
    total = ((total[: width // 2] + total[width // 2 :]) * scale).astype(BF16)
    count = total.shape[1] // LANES
    pieces = [total[:, n * LANES : (n + 1) * LANES] for n in range(count)]
    for index in range(2):
        rest = own_ref[index] + got_ref[index]
        for _ in range(3):
            piece = rest.astype(BF16)
            pieces.append(piece)
            rest = rest - piece.astype(F32)
    for peer in range(out_ref.shape[0]):
        for n, piece in enumerate(pieces):
            out_ref[peer, n] = piece


def adam_kernel(
    scale, place_ref, fix_ref, got_ref, bits_ref, turned_ref, high_ref, back_ref, sum_ref, lhs_ref
):
    peers = got_ref.shape[0]
    mine = jnp.right_shift(place_ref[0], 1)
    first_fix, second_fix = fix_ref[0], fix_ref[1]
    tops, rests = [], []
    own = jnp.zeros(sum_ref.shape, F32)
    for n in range(peers):
        total = got_ref[0, n].astype(F32)
        for peer in range(1, peers):
            total = total + got_ref[peer, n].astype(F32)
        own = jnp.where(mine == n, total, own)
        one = got_ref[n, peers].astype(F32) + got_ref[n, peers + 1].astype(F32)
        one = one + got_ref[n, peers + 2].astype(F32)
        two = got_ref[n, peers + 3].astype(F32) + got_ref[n, peers + 4].astype(F32)
        two = two + got_ref[n, peers + 5].astype(F32)
        new_one = BETA_ONE * one + (1.0 - BETA_ONE) * total
        new_two = BETA_TWO * two + (1.0 - BETA_TWO) * total * total
        direction = new_one / first_fix / (jnp.sqrt(new_two / second_fix) + EPSILON)
        top = direction.astype(BF16).astype(F32)
        tops.append(top)
        rests.append(direction - top)
    sum_ref[...] = own
    both = jnp.concatenate([jnp.concatenate(tops, axis=1), jnp.concatenate(rests, axis=1)], axis=0)
    wides = lhs_ref.shape[0]

    def fill(wide, carry):
        lhs_ref[wide] = (both * high_ref[pl.ds(wide, 1), :]).astype(BF16)
        return carry

    lax.fori_loop(0, wides, fill, 0, unroll=8)
    lhs = lhs_ref[...].reshape(wides * lhs_ref.shape[1], lhs_ref.shape[2])
    back = jnp.dot(lhs, turned_ref[...], preferred_element_type=F32)
    back = back.reshape(wides, 2, back.shape[0] // wides // 2, WIDE)
    back = back[:, 0] + back[:, 1]
    back = jnp.stack([back[:, :, :LANES], back[:, :, LANES:]], axis=1)
    back = back.reshape(2 * wides, back.shape[2], LANES)
    signs = (1 - 2 * bits_ref[...]).astype(F32) * scale
    back = (back * signs[:, None, :]).astype(BF16)
    for core in range(2):
        back_ref[:, core] = back


def expand_kernel(scale, columns_ref, turned_ref, high_ref, bits_ref, weight_ref, out_ref,
                  back_ref, lhs_ref):
    step = pl.program_id(0)
    rows = weight_ref.shape[0]
    stride = out_ref.shape[1]
    chunks = stride // WIDE

    @pl.when(step == 0)
    def _():
        columns = columns_ref[...].astype(F32).reshape(back_ref.shape[1], rows)
        back_ref[...] = jnp.transpose(columns).astype(BF16)

    for chunk in range(chunks):
        sign = high_ref[pl.ds(step * chunks + chunk, 1), :].astype(BF16)
        lhs_ref[chunk * rows : (chunk + 1) * rows, :] = back_ref[...] * sign
    update = jnp.dot(lhs_ref[...], turned_ref[...], preferred_element_type=F32)
    tiles = stride // LANES
    signs = (1 - 2 * bits_ref[pl.ds(step * tiles, tiles), :]).astype(F32) * scale
    for chunk in range(chunks):
        lanes = pl.ds(pl.multiple_of(step * stride + chunk * WIDE, WIDE), WIDE)
        moved = update[chunk * rows : (chunk + 1) * rows, :] * wide_rows(signs, 2 * chunk, 2)
        moved = weight_ref[:, lanes].astype(F32) - moved
        out_ref[:, chunk * WIDE : (chunk + 1) * WIDE] = moved.astype(BF16)


def shaped(shape, dtype):
    return jax.ShapeDtypeStruct(shape, dtype)


SMEM = pl.BlockSpec(memory_space=pltpu.SMEM)
ROOM = pltpu.CompilerParams(vmem_limit_bytes=24 << 20)
VMEM = pl.BlockSpec(memory_space=pltpu.VMEM)


def cost(flops, moved):
    return pl.CostEstimate(flops=flops, bytes_accessed=moved, transcendentals=0)


def local(replica_grads, weight, moment_one, moment_two, sign_bits, kept_rows, step_count):
    reps, panels = lax.axis_size("rep"), lax.axis_size("fsdp")
    full_len, kept_len = sign_bits.shape[0], kept_rows.shape[0]
    rows = weight.shape[0]
    peers = reps // 2
    half_width = kept_len // panels // 2
    norm_scale = 1.0 / math.sqrt(kept_len)
    place = lax.axis_index("rep").astype(jnp.int32).reshape(1)
    half = jnp.bitwise_and(place[0], 1)
    kept = kept_rows.reshape(kept_len // LANES, LANES)
    bits = sign_bits.reshape(full_len // LANES, LANES)
    one_t, two_t = moment_one.T, moment_two.T
    swap = [(n, n ^ 1) for n in range(reps)]
    wide_count = full_len // WIDE
    low_table, high_table = shaped((WIDE, kept_len), BF16), shaped((wide_count, kept_len), F32)
    half_moments = shaped((2, half_width, LANES), F32)
    everywhere = pl.BlockSpec(memory_space=pl.ANY)
    chips = [
        [(2 * chip + core) * panels + panel for panel in range(panels) for core in (0, 1)]
        for chip in range(peers)
    ]
    cores = [list(range(core, reps, 2)) for core in (0, 1)]

    def turn(when):
        return pl.pallas_call(
            turned_kernel,
            out_shape=(shaped((kept_len, WIDE), BF16), high_table),
            in_specs=[VMEM, everywhere],
            out_specs=(VMEM,) * 2,
            scratch_shapes=[pltpu.VMEM(low_table.shape, BF16)],
            compiler_params=ROOM,
            cost_estimate=cost(10 * LANES * kept_len, 8 * WIDE * kept_len),
        )(kept, when)

    def regroup(blocks):
        return lax.all_to_all(
            blocks, ("rep", "fsdp"), 0, 0, axis_index_groups=chips, tiled=True
        )

    columns = pl.pallas_call(
        functools.partial(project_kernel, norm_scale),
        out_shape=shaped((2 * panels, half_width, rows), BF16),
        in_specs=[VMEM, VMEM, pl.BlockSpec(memory_space=pltpu.HBM)],
        out_specs=VMEM,
        scratch_shapes=[
            pltpu.VMEM(low_table.shape, BF16),
            pltpu.VMEM(high_table.shape, F32),
            pltpu.VMEM((rows, full_len), BF16),
            pltpu.VMEM((rows, kept_len), F32),
            pltpu.SemaphoreType.DMA((full_len // STEP,)),
        ],
        compiler_params=ROOM,
        cost_estimate=cost(2 * rows * full_len * kept_len, 2 * rows * full_len),
    )(*(pltpu.with_memory_space_constraint(x, pltpu.HBM) for x in (kept, bits, replica_grads)))
    low, high, send_moments, own_moments = pl.pallas_call(
        tables_kernel,
        out_shape=(low_table, high_table, half_moments, half_moments),
        in_specs=[SMEM] + [VMEM] * 3 + [everywhere],
        out_specs=(VMEM,) * 4,
        compiler_params=ROOM,
        cost_estimate=cost(10 * LANES * kept_len, 8 * WIDE * kept_len),
    )(place, kept, one_t, two_t, columns)
    got_moments = lax.ppermute(send_moments, "rep", swap)
    columns = regroup(columns)

    message = pl.pallas_call(
        functools.partial(compress_kernel, norm_scale),
        out_shape=shaped((peers, kept_len // LANES + 6, half_width, LANES), BF16),
        in_specs=[VMEM] * 6,
        out_specs=VMEM,
        scratch_shapes=[pltpu.VMEM((panels // 2, 2 * half_width, kept_len), F32)],
        compiler_params=ROOM,
        cost_estimate=cost(2 * full_len * half_width * kept_len // panels, 2 * full_len * half_width),
    )(columns, bits, low, high, own_moments, got_moments)
    turned, high = turn(message)
    message = lax.all_to_all(message, "rep", 0, 0, axis_index_groups=cores)

    steps_done = step_count.astype(F32)
    fixes = jnp.stack(
        [1.0 - jnp.power(F32(BETA_ONE), steps_done), 1.0 - jnp.power(F32(BETA_TWO), steps_done)]
    )
    back, own_sum = pl.pallas_call(
        functools.partial(adam_kernel, norm_scale),
        out_shape=(
            shaped((panels, 2, half_width, rows), BF16),
            shaped((half_width, LANES), F32),
        ),
        in_specs=[SMEM, SMEM] + [VMEM] * 4,
        out_specs=(VMEM,) * 2,
        scratch_shapes=[pltpu.VMEM((wide_count, 2 * half_width, kept_len), BF16)],
        compiler_params=ROOM,
        cost_estimate=cost(4 * full_len * half_width * kept_len, 2 * full_len * half_width),
    )(place, fixes, message, bits, turned, high)
    turned, high = turn(back)
    other_sum = lax.ppermute(own_sum, "rep", swap)
    back = regroup(back.reshape(2 * panels, half_width, rows))

    row_count = moment_one.shape[0]
    own_rows = jnp.where(half == 0, own_sum[:, :row_count], own_sum[:, row_count:])
    other_rows = jnp.where(half == 0, other_sum[:, :row_count], other_sum[:, row_count:])
    compressed = jnp.where(
        half == 0,
        jnp.concatenate([own_rows, other_rows], axis=0),
        jnp.concatenate([other_rows, own_rows], axis=0),
    )
    new_one = (BETA_ONE * one_t + (1.0 - BETA_ONE) * compressed).T
    new_two = (BETA_TWO * two_t + (1.0 - BETA_TWO) * compressed * compressed).T

    new_weight = pl.pallas_call(
        functools.partial(expand_kernel, LEARN_RATE * norm_scale),
        grid=(full_len // LONG_STEP,),
        out_shape=shaped(weight.shape, BF16),
        in_specs=[VMEM] * 5,
        out_specs=pl.BlockSpec((rows, LONG_STEP), lambda i: (0, i)),
        scratch_shapes=[
            pltpu.VMEM((rows, kept_len), BF16),
            pltpu.VMEM((rows * LONG_STEP // WIDE, kept_len), BF16),
        ],
        compiler_params=ROOM,
        cost_estimate=cost(2 * rows * full_len * kept_len, 4 * rows * full_len),
    )(back, turned, high, bits, weight)
    return (new_weight, new_one, new_two)


def solution(mesh):
    in_specs = (
        P("rep", "fsdp", None),
        P("fsdp", None),
        P("rep", "fsdp"),
        P("rep", "fsdp"),
        P(),
        P(),
        P(),
    )
    out_specs = (P("fsdp", None), P("rep", "fsdp"), P("rep", "fsdp"))
    return jax.shard_map(local, mesh=mesh, in_specs=in_specs, out_specs=out_specs, check_vma=False)
```

```python
import functools
import math

import jax
import jax.numpy as jnp
from jax import lax
from jax.experimental import pallas as pl
from jax.experimental.pallas import tpu as pltpu
from jax.sharding import PartitionSpec as P

BETA_ONE = 0.9
BETA_TWO = 0.95
EPSILON = 1e-08
LEARN_RATE = 0.25
LANES = 128
WIDE = 256
STEP = 1024
LONG_STEP = 2048
SIDE = 4
F32 = jnp.float32
BF16 = jnp.bfloat16


def parity_signs(left, right):
    both = jnp.bitwise_and(left, right)
    for shift in (4, 2, 1):
        both = jnp.bitwise_xor(both, jnp.right_shift(both, shift))
    return (1 - 2 * jnp.bitwise_and(both, 1)).astype(F32)


def iota(shape, dim):
    return lax.broadcasted_iota(jnp.int32, shape, dim)


def wide_rows(rows, first, count):
    return jnp.concatenate([rows[first + n : first + n + 1, :] for n in range(count)], axis=1)


def fill_low_table(ref, columns):
    count = 16
    shape = (count, columns.shape[1])
    fine = parity_signs(iota(shape, 0), columns)
    coarse = parity_signs(iota(shape, 0), jnp.right_shift(columns, 4))
    for n in range(ref.shape[0] // count):
        ref[n * count : (n + 1) * count, :] = (fine * coarse[n : n + 1, :]).astype(BF16)


def fill_tables(kept, low_ref, high_ref):
    rows = wide_rows(kept, 0, kept.shape[0])
    fill_low_table(low_ref, rows)
    high_ref[...] = parity_signs(iota(high_ref.shape, 0), jnp.right_shift(rows, 8))


def project_kernel(scale, kept_ref, bits_ref, x_ref, out_ref, low_ref, high_ref, raw_ref, acc_ref, sems):
    rows, width = acc_ref.shape
    chunks = STEP // WIDE
    tiles = STEP // LANES

    def fetch(step):
        lanes = pl.ds(pl.multiple_of(step * STEP, STEP), STEP)
        return pltpu.make_async_copy(x_ref.at[0, :, lanes], raw_ref.at[:, lanes], sems.at[step])

    steps = raw_ref.shape[1] // STEP
    for step in range(steps):
        fetch(step).start()
    fill_tables(kept_ref[...], low_ref, high_ref)
    acc_ref[...] = jnp.zeros_like(acc_ref)

    def add(step, carry):
        fetch(step).wait()
        signs = (1 - 2 * bits_ref[pl.ds(step * tiles, tiles), :]).astype(F32)
        pieces = []
        for n in range(chunks):
            lanes = pl.ds(pl.multiple_of(step * STEP + n * WIDE, WIDE), WIDE)
            pieces.append(raw_ref[:, lanes] * wide_rows(signs, 2 * n, 2).astype(BF16))
        stacked = jnp.concatenate(pieces, axis=0)
        for first in range(0, width, WIDE):
            columns = slice(first, first + WIDE)
            part = jnp.dot(stacked, low_ref[:, columns], preferred_element_type=F32)
            total = acc_ref[:, columns]
            for n in range(chunks):
                sign = high_ref[pl.ds(step * chunks + n, 1), columns]
                total = total + part[n * rows : (n + 1) * rows, :] * sign
            acc_ref[:, columns] = total
        return carry

    lax.fori_loop(0, steps, add, 0)
    done = jnp.transpose(acc_ref[...] * scale)
    out_ref[...] = done.reshape(out_ref.shape).astype(out_ref.dtype)


def tables_kernel(kept_ref, one_ref, two_ref, when_ref, low_ref, high_ref, moments_ref):
    fill_tables(kept_ref[...], low_ref, high_ref)
    moments_ref[...] = jnp.concatenate([one_ref[...], two_ref[...]], axis=1)


def turned_kernel(kept_ref, when_ref, turned_ref, high_ref, low_ref):
    fill_tables(kept_ref[...], low_ref, high_ref)
    turned_ref[...] = jnp.transpose(low_ref[...].astype(F32)).astype(BF16)


def compress_kernel(
    scale, panel_ref, y_ref, bits_ref, low_ref, high_ref, moments_ref, out_ref, part_ref
):
    sources, width, lanes = y_ref.shape
    line = sources // SIDE
    place = panel_ref[0] // line
    signs = bits_ref[pl.ds(pl.multiple_of(place * line, line), line), :]
    signs = (1 - 2 * signs).astype(F32)
    y = y_ref[...].astype(F32).reshape(SIDE, line, width, lanes) * signs[None, :, None, :]
    y = y.reshape(sources // 2, 2, width, lanes)
    y = jnp.concatenate([y[:, 0], y[:, 1]], axis=2).reshape(sources // 2 * width, 2 * lanes)
    part = jnp.dot(y.astype(BF16), low_ref[...], preferred_element_type=F32)
    part_ref[...] = part.reshape(part_ref.shape)
    total = jnp.zeros(part_ref.shape[2:], F32)
    for pair in range(line // 2):
        one = part_ref[0, pair]
        for other in range(1, SIDE):
            one = one + part_ref[other, pair]
        total = total + one * high_ref[pl.ds(place * (line // 2) + pair, 1), :]
    total = (total * scale).astype(BF16).astype(F32)
    pieces = [total[:, n : n + LANES] for n in range(0, total.shape[1], LANES)]
    rest = moments_ref[...]
    for _ in range(3):
        piece = rest.astype(BF16).astype(F32)
        pieces.append(piece)
        rest = rest - piece
    half = width // 2
    for core in range(2):
        for n, piece in enumerate(pieces):
            block = piece[core * half : (core + 1) * half, :].astype(BF16)
            for peer in range(out_ref.shape[0]):
                out_ref[peer, core, n] = block


def adam_kernel(
    scale, rep_ref, panel_ref, fix_ref, got_ref, bits_ref, turned_ref, high_ref,
    back_ref, sum_ref, lhs_ref,
):
    peers = got_ref.shape[0]
    line = back_ref.shape[1]
    place = panel_ref[0] // line
    mine = rep_ref[0] // (2 * SIDE) * SIDE + place
    first_fix, second_fix = fix_ref[0], fix_ref[1]
    middle = LANES // 2
    tops, rests = [], []
    own = jnp.zeros(sum_ref.shape, F32)
    for n in range(peers):
        total = jnp.zeros(sum_ref.shape, F32)
        for peer in range(peers):
            for core in range(2):
                total = total + got_ref[peer, core, n].astype(F32)
        own = jnp.where(mine == n, total, own)
        moments = []
        for core in range(2):
            moment = got_ref[n, core, peers].astype(F32) + got_ref[n, core, peers + 1].astype(F32)
            moments.append(moment + got_ref[n, core, peers + 2].astype(F32))
        one = jnp.concatenate([moments[0][:, :middle], moments[1][:, :middle]], axis=1)
        two = jnp.concatenate([moments[0][:, middle:], moments[1][:, middle:]], axis=1)
        new_one = BETA_ONE * one + (1.0 - BETA_ONE) * total
        new_two = BETA_TWO * two + (1.0 - BETA_TWO) * total * total
        direction = new_one / first_fix / (jnp.sqrt(new_two / second_fix) + EPSILON)
        top = direction.astype(BF16).astype(F32)
        tops.append(top)
        rests.append(direction - top)
    sum_ref[...] = own
    both = jnp.concatenate([jnp.concatenate(tops, axis=1), jnp.concatenate(rests, axis=1)], axis=0)
    wides = lhs_ref.shape[0]
    for wide in range(wides):
        lhs_ref[wide] = (both * high_ref[pl.ds(place * wides + wide, 1), :]).astype(BF16)
    lhs = lhs_ref[...].reshape(wides * lhs_ref.shape[1], lhs_ref.shape[2])
    back = jnp.dot(lhs, turned_ref[...], preferred_element_type=F32)
    back = back.reshape(wides, 2, back.shape[0] // wides // 2, WIDE)
    back = back[:, 0] + back[:, 1]
    back = jnp.stack([back[:, :, :LANES], back[:, :, LANES:]], axis=1)
    back = back.reshape(2 * wides, back.shape[2], LANES)
    signs = bits_ref[pl.ds(pl.multiple_of(place * line, line), line), :]
    signs = (1 - 2 * signs).astype(F32) * scale
    back = (back * signs[:, None, :]).astype(BF16)
    for copy in range(SIDE):
        back_ref[copy] = back


def expand_kernel(
    scale, rep_ref, own_ref, other_ref, turned_ref, high_ref, bits_ref, weight_ref, out_ref,
    both_ref, back_ref, lhs_ref,
):
    step = pl.program_id(0)
    rows = weight_ref.shape[0]
    stride = out_ref.shape[1]
    chunks = stride // WIDE

    @pl.when(step == 0)
    def _():
        core = jnp.bitwise_and(rep_ref[0], 1)
        both_ref[:, pl.ds(core, 1)] = own_ref[...].astype(F32)[:, None]
        both_ref[:, pl.ds(1 - core, 1)] = other_ref[...].astype(F32)[:, None]
        columns = both_ref[...].reshape(back_ref.shape[1], rows)
        back_ref[...] = jnp.transpose(columns).astype(BF16)

    for chunk in range(chunks):
        sign = high_ref[pl.ds(step * chunks + chunk, 1), :].astype(BF16)
        lhs_ref[chunk * rows : (chunk + 1) * rows, :] = back_ref[...] * sign
    update = jnp.dot(lhs_ref[...], turned_ref[...], preferred_element_type=F32)
    tiles = stride // LANES
    signs = (1 - 2 * bits_ref[pl.ds(step * tiles, tiles), :]).astype(F32) * scale
    for chunk in range(chunks):
        lanes = pl.ds(pl.multiple_of(step * stride + chunk * WIDE, WIDE), WIDE)
        moved = update[chunk * rows : (chunk + 1) * rows, :] * wide_rows(signs, 2 * chunk, 2)
        moved = weight_ref[:, lanes].astype(F32) - moved
        out_ref[:, chunk * WIDE : (chunk + 1) * WIDE] = moved.astype(BF16)


def shaped(shape, dtype):
    return jax.ShapeDtypeStruct(shape, dtype)


SMEM = pl.BlockSpec(memory_space=pltpu.SMEM)
ROOM = pltpu.CompilerParams(vmem_limit_bytes=24 << 20)
VMEM = pl.BlockSpec(memory_space=pltpu.VMEM)


def cost(flops, moved):
    return pl.CostEstimate(flops=flops, bytes_accessed=moved, transcendentals=0)


def local(replica_grads, weight, moment_one, moment_two, sign_bits, kept_rows, step_count):
    reps, panels = lax.axis_size("rep"), lax.axis_size("fsdp")
    full_len, kept_len = sign_bits.shape[0], kept_rows.shape[0]
    rows = weight.shape[0]
    peers = reps // 2
    half_width = kept_len // panels // 2
    norm_scale = 1.0 / math.sqrt(kept_len)
    rep = lax.axis_index("rep").astype(jnp.int32).reshape(1)
    panel = lax.axis_index("fsdp").astype(jnp.int32).reshape(1)
    core = jnp.bitwise_and(rep[0], 1)
    kept = kept_rows.reshape(kept_len // LANES, LANES)
    bits = sign_bits.reshape(full_len // LANES, LANES)
    one_t, two_t = moment_one.T, moment_two.T
    wide_count = full_len // WIDE
    low_table, high_table = shaped((WIDE, kept_len), BF16), shaped((wide_count, kept_len), F32)
    everywhere = pl.BlockSpec(memory_space=pl.ANY)
    both = ("rep", "fsdp")
    line, far = panels // SIDE, peers // SIDE
    near = range(SIDE)

    def device(y_hi, x, side, y_lo, z):
        return ((y_hi * SIDE + x) * 2 + side) * panels + y_lo * line + z

    planes = [
        [device(y_hi, x, side, y_lo, z) for x in near for z in range(line)]
        for y_hi in range(far) for side in range(2) for y_lo in near
    ]
    columns_of_chips = [
        [device(y_hi, x, side, y_lo, z) for y_hi in range(far) for y_lo in near for side in range(2)]
        for x in near for z in range(line)
    ]

    def turn_over(cross):
        return [
            (device(y_hi, x, side, y_lo, z), device(y_hi, y_lo, side ^ cross, x, z))
            for y_hi in range(far) for x in near for side in range(2)
            for y_lo in near for z in range(line)
        ]

    def turn(when):
        return pl.pallas_call(
            turned_kernel,
            out_shape=(shaped((kept_len, WIDE), BF16), high_table),
            in_specs=[VMEM, everywhere],
            out_specs=(VMEM,) * 2,
            scratch_shapes=[pltpu.VMEM(low_table.shape, BF16)],
            compiler_params=ROOM,
            cost_estimate=cost(10 * LANES * kept_len, 8 * WIDE * kept_len),
        )(kept, when)

    def regroup(blocks, groups):
        return lax.all_to_all(blocks, both, 0, 0, axis_index_groups=groups, tiled=True)

    columns = pl.pallas_call(
        functools.partial(project_kernel, norm_scale),
        out_shape=shaped((panels, 2 * half_width, rows), BF16),
        in_specs=[VMEM, VMEM, pl.BlockSpec(memory_space=pltpu.HBM)],
        out_specs=VMEM,
        scratch_shapes=[
            pltpu.VMEM(low_table.shape, BF16),
            pltpu.VMEM(high_table.shape, F32),
            pltpu.VMEM((rows, full_len), BF16),
            pltpu.VMEM((rows, kept_len), F32),
            pltpu.SemaphoreType.DMA((full_len // STEP,)),
        ],
        compiler_params=ROOM,
        cost_estimate=cost(2 * rows * full_len * kept_len, 2 * rows * full_len),
    )(*(pltpu.with_memory_space_constraint(x, pltpu.HBM) for x in (kept, bits, replica_grads)))
    low, high, moments = pl.pallas_call(
        tables_kernel,
        out_shape=(low_table, high_table, shaped((2 * half_width, LANES), F32)),
        in_specs=[VMEM] * 3 + [everywhere],
        out_specs=(VMEM,) * 3,
        compiler_params=ROOM,
        cost_estimate=cost(10 * LANES * kept_len, 8 * WIDE * kept_len),
    )(kept, one_t, two_t, columns)
    moments = lax.ppermute(moments, both, turn_over(0))
    columns = regroup(columns, planes)

    pieces = kept_len // LANES + 3
    message_shape = (peers, 2, pieces, half_width, LANES)
    message = pl.pallas_call(
        functools.partial(compress_kernel, norm_scale),
        out_shape=shaped(message_shape, BF16),
        in_specs=[SMEM] + [VMEM] * 5,
        out_specs=VMEM,
        scratch_shapes=[pltpu.VMEM((SIDE, line // 2, 2 * half_width, kept_len), F32)],
        compiler_params=ROOM,
        cost_estimate=cost(2 * full_len * half_width * kept_len // panels, 2 * full_len * half_width),
    )(panel, columns, bits, low, high, moments)
    turned, high = turn(message)
    message = regroup(message.reshape((2 * peers,) + message_shape[2:]), columns_of_chips)
    message = message.reshape(message_shape)

    steps_done = step_count.astype(F32)
    fixes = jnp.stack(
        [1.0 - jnp.power(F32(BETA_ONE), steps_done), 1.0 - jnp.power(F32(BETA_TWO), steps_done)]
    )
    back, own_sum = pl.pallas_call(
        functools.partial(adam_kernel, norm_scale),
        out_shape=(
            shaped((SIDE, line, half_width, rows), BF16),
            shaped((half_width, LANES), F32),
        ),
        in_specs=[SMEM] * 3 + [VMEM] * 4,
        out_specs=(VMEM,) * 2,
        scratch_shapes=[pltpu.VMEM((line // 2, 2 * half_width, kept_len), BF16)],
        compiler_params=ROOM,
        cost_estimate=cost(full_len * half_width * kept_len, 2 * full_len * half_width),
    )(rep, panel, fixes, message, bits, turned, high)
    turned, high = turn(back)
    same_sum = lax.ppermute(own_sum, both, turn_over(0))
    cross_sum = lax.ppermute(own_sum, both, turn_over(1))
    back = regroup(back.reshape(panels, half_width, rows), planes)
    other_back = lax.ppermute(back, "rep", [(n, n ^ 1) for n in range(reps)])

    row_count = moment_one.shape[0]
    same_rows = jnp.where(core == 0, same_sum[:, :row_count], same_sum[:, row_count:])
    cross_rows = jnp.where(core == 0, cross_sum[:, :row_count], cross_sum[:, row_count:])
    compressed = jnp.where(
        core == 0,
        jnp.concatenate([same_rows, cross_rows], axis=0),
        jnp.concatenate([cross_rows, same_rows], axis=0),
    )
    new_one = (BETA_ONE * one_t + (1.0 - BETA_ONE) * compressed).T
    new_two = (BETA_TWO * two_t + (1.0 - BETA_TWO) * compressed * compressed).T

    new_weight = pl.pallas_call(
        functools.partial(expand_kernel, LEARN_RATE * norm_scale),
        grid=(full_len // LONG_STEP,),
        out_shape=shaped(weight.shape, BF16),
        in_specs=[SMEM] + [VMEM] * 6,
        out_specs=pl.BlockSpec((rows, LONG_STEP), lambda i: (0, i)),
        scratch_shapes=[
            pltpu.VMEM((panels, 2, half_width, rows), F32),
            pltpu.VMEM((rows, kept_len), BF16),
            pltpu.VMEM((rows * LONG_STEP // WIDE, kept_len), BF16),
        ],
        compiler_params=ROOM,
        cost_estimate=cost(2 * rows * full_len * kept_len, 4 * rows * full_len),
    )(rep, back, other_back, turned, high, bits, weight)
    return (new_weight, new_one, new_two)


def solution(mesh):
    in_specs = (
        P("rep", "fsdp", None),
        P("fsdp", None),
        P("rep", "fsdp"),
        P("rep", "fsdp"),
        P(),
        P(),
        P(),
    )
    out_specs = (P("fsdp", None), P("rep", "fsdp"), P("rep", "fsdp"))
    return jax.shard_map(local, mesh=mesh, in_specs=in_specs, out_specs=out_specs, check_vma=False)
```

```python
import functools
import math

import jax
import jax.numpy as jnp
from jax import lax
from jax.experimental import pallas as pl
from jax.experimental.pallas import tpu as pltpu
from jax.sharding import PartitionSpec as P

BETA_ONE = 0.9
BETA_TWO = 0.95
EPSILON = 1e-08
LEARN_RATE = 0.25
LANES = 128
WIDE = 256
STEP = 1024
LONG_STEP = 2048
SIDE = 4
PIECES = 2
F32 = jnp.float32
BF16 = jnp.bfloat16


def parity_signs(left, right):
    both = jnp.bitwise_and(left, right)
    for shift in (4, 2, 1):
        both = jnp.bitwise_xor(both, jnp.right_shift(both, shift))
    return (1 - 2 * jnp.bitwise_and(both, 1)).astype(F32)


def iota(shape, dim):
    return lax.broadcasted_iota(jnp.int32, shape, dim)


def wide_rows(rows, first, count):
    return jnp.concatenate([rows[first + n : first + n + 1, :] for n in range(count)], axis=1)


def fill_low_table(ref, columns):
    count = 16
    shape = (count, columns.shape[1])
    fine = parity_signs(iota(shape, 0), columns)
    coarse = parity_signs(iota(shape, 0), jnp.right_shift(columns, 4))
    for n in range(ref.shape[0] // count):
        ref[n * count : (n + 1) * count, :] = (fine * coarse[n : n + 1, :]).astype(BF16)


def fill_tables(kept, low_ref, high_ref):
    rows = wide_rows(kept, 0, kept.shape[0])
    fill_low_table(low_ref, rows)
    high_ref[...] = parity_signs(iota(high_ref.shape, 0), jnp.right_shift(rows, 8))


def order_columns(half, kept):
    blocks = kept.shape[0]
    digits = jnp.concatenate([jnp.right_shift(kept, 7), jnp.bitwise_and(kept, LANES - 1)], axis=0)
    digits = digits.astype(F32).astype(BF16)
    source, target = iota((LANES, LANES), 0), iota((LANES, LANES), 1)
    same = jnp.logical_and(
        jnp.right_shift(source, 4) == jnp.bitwise_and(jnp.right_shift(target, 3), 7),
        jnp.bitwise_and(source, 7) == jnp.bitwise_and(target, 7),
    )
    source_half = jnp.bitwise_and(jnp.right_shift(source, 3), 1)
    pieces = []
    for wanted in (1 - half, half):
        moved = []
        for part in (0, 1):
            pick = jnp.logical_and(same, source_half == wanted)
            pick = jnp.logical_and(pick, jnp.right_shift(target, 6) == part)
            pick = jnp.where(pick, 1.0, 0.0).astype(BF16)
            moved.append(jnp.dot(digits, pick, preferred_element_type=F32))
        for pair in range(blocks // 2):
            even, odd = 2 * pair, 2 * pair + 1
            top = moved[0][even : even + 1, :] + moved[1][odd : odd + 1, :]
            low = (
                moved[0][blocks + even : blocks + even + 1, :]
                + moved[1][blocks + odd : blocks + odd + 1, :]
            )
            pieces.append(top * LANES + low)
    return jnp.concatenate(pieces, axis=1).astype(jnp.int32)


def project_half(scale, first, x_of, low_ref, high_ref, out_ref, acc_ref):
    rows, width = acc_ref.shape
    chunks = STEP // WIDE
    columns = slice(first, first + width)
    acc_ref[...] = jnp.zeros_like(acc_ref)

    def add(step, carry):
        x = x_of(step)
        stacked = jnp.concatenate([x[:, n * WIDE : (n + 1) * WIDE] for n in range(chunks)], axis=0)
        part = jnp.dot(stacked, low_ref[:, columns], preferred_element_type=F32)
        total = acc_ref[...]
        for n in range(chunks):
            sign = high_ref[pl.ds(step * chunks + n, 1), columns]
            total = total + part[n * rows : (n + 1) * rows, :] * sign
        acc_ref[...] = total
        return carry

    steps = high_ref.shape[0] // chunks
    lax.fori_loop(0, steps, add, 0)
    done = jnp.transpose(acc_ref[...] * scale)
    out_ref[...] = done.reshape(out_ref.shape).astype(out_ref.dtype)


def project_other_kernel(
    scale, rep_ref, kept_ref, bits_ref, x_ref, low_ref, high_ref, signed_ref, out_ref, acc_ref, sems
):
    def fetch(step):
        lanes = pl.ds(pl.multiple_of(step * STEP, STEP), STEP)
        return pltpu.make_async_copy(x_ref.at[0, :, lanes], signed_ref.at[:, lanes], sems.at[step])

    for step in range(signed_ref.shape[1] // STEP):
        fetch(step).start()
    half = jnp.bitwise_and(rep_ref[0], 1)
    columns = order_columns(half, kept_ref[...])
    fill_low_table(low_ref, columns)
    high_ref[...] = parity_signs(iota(high_ref.shape, 0), jnp.right_shift(columns, 8))
    def x_of(step):
        fetch(step).wait()
        lanes = pl.ds(pl.multiple_of(step * STEP, STEP), STEP)
        signs = (1 - 2 * bits_ref[pl.ds(step * (STEP // LANES), STEP // LANES), :]).astype(F32)
        x = signed_ref[:, lanes] * wide_rows(signs, 0, STEP // LANES).astype(BF16)
        signed_ref[:, lanes] = x
        return x

    project_half(scale, 0, x_of, low_ref, high_ref, out_ref, acc_ref)


def project_own_kernel(scale, signed_ref, low_ref, high_ref, out_ref, acc_ref):
    def x_of(step):
        return signed_ref[:, pl.ds(pl.multiple_of(step * STEP, STEP), STEP)]

    project_half(scale, acc_ref.shape[1], x_of, low_ref, high_ref, out_ref, acc_ref)


def tables_kernel(rep_ref, kept_ref, one_ref, two_ref, when_ref, low_ref, high_ref, same_ref, cross_ref):
    fill_tables(kept_ref[...], low_ref, high_ref)
    core = jnp.bitwise_and(rep_ref[0], 1)
    both = jnp.concatenate([one_ref[...], two_ref[...]], axis=1)
    half = both.shape[0] // 2
    upper, lower = both[:half, :], both[half:, :]
    same_ref[...] = jnp.where(core == 0, upper, lower)
    cross_ref[...] = jnp.where(core == 0, lower, upper)


def turned_kernel(kept_ref, when_ref, turned_ref, high_ref, low_ref):
    fill_tables(kept_ref[...], low_ref, high_ref)
    turned_ref[...] = jnp.transpose(low_ref[...].astype(F32)).astype(BF16)


def compress_kernel(
    scale, rep_ref, panel_ref, y_ref, bits_ref, low_ref, high_ref, same_ref, cross_ref,
    out_ref, part_ref,
):
    sources, width, lanes = y_ref.shape
    line = sources // SIDE
    place = panel_ref[0] // line
    signs = bits_ref[pl.ds(pl.multiple_of(place * line, line), line), :]
    signs = (1 - 2 * signs).astype(F32)
    y = y_ref[...].astype(F32).reshape(SIDE, line, width, lanes) * signs[None, :, None, :]
    y = y.reshape(sources // 2, 2, width, lanes)
    y = jnp.concatenate([y[:, 0], y[:, 1]], axis=2).reshape(sources // 2 * width, 2 * lanes)
    part = jnp.dot(y.astype(BF16), low_ref[...], preferred_element_type=F32)
    part_ref[...] = part.reshape(part_ref.shape)
    total = jnp.zeros(part_ref.shape[2:], F32)
    for pair in range(line // 2):
        one = part_ref[0, pair]
        for other in range(1, SIDE):
            one = one + part_ref[other, pair]
        total = total + one * high_ref[pl.ds(place * (line // 2) + pair, 1), :]
    total = (total * scale).astype(BF16)
    pieces = [total[:, n : n + LANES] for n in range(0, total.shape[1], LANES)]
    core = jnp.bitwise_and(rep_ref[0], 1)
    same, cross = same_ref[...], cross_ref[...]
    first, second = jnp.where(core == 0, same, cross), jnp.where(core == 0, cross, same)
    middle = LANES // 2
    for lanes in (slice(0, middle), slice(middle, LANES)):
        rest = jnp.concatenate([first[:, lanes], second[:, lanes]], axis=1)
        for _ in range(PIECES):
            piece = rest.astype(BF16)
            pieces.append(piece)
            rest = rest - piece.astype(F32)
    for n, piece in enumerate(pieces):
        for peer in range(out_ref.shape[0]):
            out_ref[peer, n] = piece


def adam_kernel(
    scale, rep_ref, panel_ref, fix_ref, got_ref, bits_ref, turned_ref, high_ref,
    back_ref, sum_ref, lhs_ref,
):
    peers = got_ref.shape[0]
    line = back_ref.shape[1]
    place = panel_ref[0] // line
    mine = rep_ref[0] // (2 * SIDE) * SIDE + place
    first_fix, second_fix = fix_ref[0], fix_ref[1]
    tops, rests = [], []
    own = jnp.zeros(sum_ref.shape, F32)
    for n in range(peers):
        total = jnp.zeros(sum_ref.shape, F32)
        for peer in range(peers):
            total = total + got_ref[peer, n].astype(F32)
        own = jnp.where(mine == n, total, own)
        moments = []
        for index in range(2):
            moment = jnp.zeros(sum_ref.shape, F32)
            for piece in reversed(range(PIECES)):
                moment = moment + got_ref[n, peers + index * PIECES + piece].astype(F32)
            moments.append(moment)
        one, two = moments
        new_one = BETA_ONE * one + (1.0 - BETA_ONE) * total
        new_two = BETA_TWO * two + (1.0 - BETA_TWO) * total * total
        direction = new_one / first_fix / (jnp.sqrt(new_two / second_fix) + EPSILON)
        top = direction.astype(BF16).astype(F32)
        tops.append(top)
        rests.append(direction - top)
    sum_ref[...] = own
    both = jnp.concatenate([jnp.concatenate(tops, axis=1), jnp.concatenate(rests, axis=1)], axis=0)
    wides = lhs_ref.shape[0]
    for wide in range(wides):
        lhs_ref[wide] = (both * high_ref[pl.ds(place * wides + wide, 1), :]).astype(BF16)
    lhs = lhs_ref[...].reshape(wides * lhs_ref.shape[1], lhs_ref.shape[2])
    back = jnp.dot(lhs, turned_ref[...], preferred_element_type=F32)
    back = back.reshape(wides, 2, back.shape[0] // wides // 2, WIDE)
    back = back[:, 0] + back[:, 1]
    back = jnp.stack([back[:, :, :LANES], back[:, :, LANES:]], axis=1)
    back = back.reshape(2 * wides, back.shape[2], LANES)
    signs = bits_ref[pl.ds(pl.multiple_of(place * line, line), line), :]
    signs = (1 - 2 * signs).astype(F32) * scale
    back = (back * signs[:, None, :]).astype(BF16)
    for copy in range(SIDE):
        back_ref[copy] = back


def expand_kernel(
    scale, rep_ref, own_ref, other_ref, turned_ref, high_ref, bits_ref, weight_ref, out_ref,
    both_ref, back_ref, lhs_ref,
):
    step = pl.program_id(0)
    rows = weight_ref.shape[0]
    stride = out_ref.shape[1]
    chunks = stride // WIDE

    @pl.when(step == 0)
    def _():
        core = jnp.bitwise_and(rep_ref[0], 1)
        both_ref[:, pl.ds(core, 1)] = own_ref[...].astype(F32)[:, None]
        both_ref[:, pl.ds(1 - core, 1)] = other_ref[...].astype(F32)[:, None]
        columns = both_ref[...].reshape(back_ref.shape[1], rows)
        back_ref[...] = jnp.transpose(columns).astype(BF16)

    for chunk in range(chunks):
        sign = high_ref[pl.ds(step * chunks + chunk, 1), :].astype(BF16)
        lhs_ref[chunk * rows : (chunk + 1) * rows, :] = back_ref[...] * sign
    update = jnp.dot(lhs_ref[...], turned_ref[...], preferred_element_type=F32)
    tiles = stride // LANES
    signs = (1 - 2 * bits_ref[pl.ds(step * tiles, tiles), :]).astype(F32) * scale
    for chunk in range(chunks):
        lanes = pl.ds(pl.multiple_of(step * stride + chunk * WIDE, WIDE), WIDE)
        moved = update[chunk * rows : (chunk + 1) * rows, :] * wide_rows(signs, 2 * chunk, 2)
        moved = weight_ref[:, lanes].astype(F32) - moved
        out_ref[:, chunk * WIDE : (chunk + 1) * WIDE] = moved.astype(BF16)


def shaped(shape, dtype):
    return jax.ShapeDtypeStruct(shape, dtype)


SMEM = pl.BlockSpec(memory_space=pltpu.SMEM)
ROOM = pltpu.CompilerParams(vmem_limit_bytes=24 << 20)
VMEM = pl.BlockSpec(memory_space=pltpu.VMEM)


def cost(flops, moved):
    return pl.CostEstimate(flops=flops, bytes_accessed=moved, transcendentals=0)


def local(replica_grads, weight, moment_one, moment_two, sign_bits, kept_rows, step_count):
    reps, panels = lax.axis_size("rep"), lax.axis_size("fsdp")
    full_len, kept_len = sign_bits.shape[0], kept_rows.shape[0]
    rows = weight.shape[0]
    peers = reps // 2
    half_width = kept_len // panels // 2
    norm_scale = 1.0 / math.sqrt(kept_len)
    rep = lax.axis_index("rep").astype(jnp.int32).reshape(1)
    panel = lax.axis_index("fsdp").astype(jnp.int32).reshape(1)
    core = jnp.bitwise_and(rep[0], 1)
    kept = kept_rows.reshape(kept_len // LANES, LANES)
    bits = sign_bits.reshape(full_len // LANES, LANES)
    one_t, two_t = moment_one.T, moment_two.T
    wide_count = full_len // WIDE
    low_table, high_table = shaped((WIDE, kept_len), BF16), shaped((wide_count, kept_len), F32)
    everywhere = pl.BlockSpec(memory_space=pl.ANY)
    both = ("rep", "fsdp")
    swap = [(n, n ^ 1) for n in range(reps)]
    line, far = panels // SIDE, peers // SIDE
    near = range(SIDE)

    def device(y_hi, x, side, y_lo, z):
        return ((y_hi * SIDE + x) * 2 + side) * panels + y_lo * line + z

    planes = [
        [device(y_hi, x, side, y_lo, z) for x in near for z in range(line)]
        for y_hi in range(far) for side in range(2) for y_lo in near
    ]
    rings = [
        [device(y_hi, x, side, y_lo, z) for y_hi in range(far) for y_lo in near]
        for x in near for side in range(2) for z in range(line)
    ]

    def turn_over(cross):
        return [
            (device(y_hi, x, side, y_lo, z), device(y_hi, y_lo, side ^ cross, x, z))
            for y_hi in range(far) for x in near for side in range(2)
            for y_lo in near for z in range(line)
        ]

    def turn(when):
        return pl.pallas_call(
            turned_kernel,
            out_shape=(shaped((kept_len, WIDE), BF16), high_table),
            in_specs=[VMEM, everywhere],
            out_specs=(VMEM,) * 2,
            scratch_shapes=[pltpu.VMEM(low_table.shape, BF16)],
            compiler_params=ROOM,
            cost_estimate=cost(10 * LANES * kept_len, 8 * WIDE * kept_len),
        )(kept, when)

    def regroup(blocks, groups):
        return lax.all_to_all(blocks, both, 0, 0, axis_index_groups=groups, tiled=True)

    half_shape = (panels, half_width, rows)
    half_len = kept_len // 2
    in_hbm = [pltpu.with_memory_space_constraint(x, pltpu.HBM) for x in (kept, bits, replica_grads)]
    col_low, col_high, signed, for_other = pl.pallas_call(
        functools.partial(project_other_kernel, norm_scale),
        out_shape=(low_table, high_table, shaped((rows, full_len), BF16), shaped(half_shape, BF16)),
        in_specs=[SMEM] + [VMEM] * 2 + [pl.BlockSpec(memory_space=pltpu.HBM)],
        out_specs=(VMEM,) * 4,
        scratch_shapes=[
            pltpu.VMEM((rows, half_len), F32),
            pltpu.SemaphoreType.DMA((full_len // STEP,)),
        ],
        compiler_params=ROOM,
        cost_estimate=cost(2 * rows * full_len * half_len, 2 * rows * full_len),
    )(rep, *in_hbm)
    from_other = lax.ppermute(for_other, "rep", swap)
    mine = pl.pallas_call(
        functools.partial(project_own_kernel, norm_scale),
        out_shape=shaped(half_shape, F32),
        in_specs=[VMEM] * 3,
        out_specs=VMEM,
        scratch_shapes=[pltpu.VMEM((rows, half_len), F32)],
        compiler_params=ROOM,
        cost_estimate=cost(2 * rows * full_len * half_len, 2 * rows * full_len),
    )(signed, col_low, col_high)
    columns = (mine + from_other.astype(F32)).astype(BF16)
    half_moments = shaped((half_width, LANES), F32)
    low, high, for_same, for_cross = pl.pallas_call(
        tables_kernel,
        out_shape=(low_table, high_table, half_moments, half_moments),
        in_specs=[SMEM] + [VMEM] * 3 + [everywhere],
        out_specs=(VMEM,) * 4,
        compiler_params=ROOM,
        cost_estimate=cost(10 * LANES * kept_len, 8 * WIDE * kept_len),
    )(rep, kept, one_t, two_t, columns)
    from_same = lax.ppermute(for_same, both, turn_over(0))
    from_cross = lax.ppermute(for_cross, both, turn_over(1))
    columns = regroup(columns, planes)

    message_shape = (peers, kept_len // LANES + 2 * PIECES, half_width, LANES)
    message = pl.pallas_call(
        functools.partial(compress_kernel, norm_scale),
        out_shape=shaped(message_shape, BF16),
        in_specs=[SMEM] * 2 + [VMEM] * 6,
        out_specs=VMEM,
        scratch_shapes=[pltpu.VMEM((SIDE, line // 2, half_width, kept_len), F32)],
        compiler_params=ROOM,
        cost_estimate=cost(2 * full_len * half_width * kept_len // panels, 2 * full_len * half_width),
    )(rep, panel, columns, bits, low, high, from_same, from_cross)
    turned, high = turn(message)
    message = regroup(message, rings)

    steps_done = step_count.astype(F32)
    fixes = jnp.stack(
        [1.0 - jnp.power(F32(BETA_ONE), steps_done), 1.0 - jnp.power(F32(BETA_TWO), steps_done)]
    )
    back, own_sum = pl.pallas_call(
        functools.partial(adam_kernel, norm_scale),
        out_shape=(
            shaped((SIDE, line, half_width, rows), BF16),
            shaped((half_width, LANES), F32),
        ),
        in_specs=[SMEM] * 3 + [VMEM] * 4,
        out_specs=(VMEM,) * 2,
        scratch_shapes=[pltpu.VMEM((line // 2, 2 * half_width, kept_len), BF16)],
        compiler_params=ROOM,
        cost_estimate=cost(full_len * half_width * kept_len, 2 * full_len * half_width),
    )(rep, panel, fixes, message, bits, turned, high)
    turned, high = turn(back)
    same_sum = lax.ppermute(own_sum, both, turn_over(0))
    cross_sum = lax.ppermute(own_sum, both, turn_over(1))
    back = regroup(back.reshape(panels, half_width, rows), planes)
    other_back = lax.ppermute(back, "rep", swap)

    row_count = moment_one.shape[0]
    same_rows = jnp.where(core == 0, same_sum[:, :row_count], same_sum[:, row_count:])
    cross_rows = jnp.where(core == 0, cross_sum[:, :row_count], cross_sum[:, row_count:])
    compressed = jnp.where(
        core == 0,
        jnp.concatenate([same_rows, cross_rows], axis=0),
        jnp.concatenate([cross_rows, same_rows], axis=0),
    )
    new_one = (BETA_ONE * one_t + (1.0 - BETA_ONE) * compressed).T
    new_two = (BETA_TWO * two_t + (1.0 - BETA_TWO) * compressed * compressed).T

    new_weight = pl.pallas_call(
        functools.partial(expand_kernel, LEARN_RATE * norm_scale),
        grid=(full_len // LONG_STEP,),
        out_shape=shaped(weight.shape, BF16),
        in_specs=[SMEM] + [VMEM] * 6,
        out_specs=pl.BlockSpec((rows, LONG_STEP), lambda i: (0, i)),
        scratch_shapes=[
            pltpu.VMEM((panels, 2, half_width, rows), F32),
            pltpu.VMEM((rows, kept_len), BF16),
            pltpu.VMEM((rows * LONG_STEP // WIDE, kept_len), BF16),
        ],
        compiler_params=ROOM,
        cost_estimate=cost(2 * rows * full_len * kept_len, 4 * rows * full_len),
    )(rep, back, other_back, turned, high, bits, weight)
    return (new_weight, new_one, new_two)


def solution(mesh):
    in_specs = (
        P("rep", "fsdp", None),
        P("fsdp", None),
        P("rep", "fsdp"),
        P("rep", "fsdp"),
        P(),
        P(),
        P(),
    )
    out_specs = (P("fsdp", None), P("rep", "fsdp"), P("rep", "fsdp"))
    return jax.shard_map(local, mesh=mesh, in_specs=in_specs, out_specs=out_specs, check_vma=False)
```

```python
import functools
import math

import jax
import jax.numpy as jnp
from jax import lax
from jax.experimental import pallas as pl
from jax.experimental.pallas import tpu as pltpu
from jax.sharding import PartitionSpec as P

BETA_ONE = 0.9
BETA_TWO = 0.95
EPSILON = 1e-08
LEARN_RATE = 0.25
LANES = 128
WIDE = 256
STEP = 1024
LONG_STEP = 2048
SIDE = 4
PIECES = 2
F32 = jnp.float32
BF16 = jnp.bfloat16


def parity_signs(left, right):
    both = jnp.bitwise_and(left, right)
    for shift in (4, 2, 1):
        both = jnp.bitwise_xor(both, jnp.right_shift(both, shift))
    return (1 - 2 * jnp.bitwise_and(both, 1)).astype(F32)


def iota(shape, dim):
    return lax.broadcasted_iota(jnp.int32, shape, dim)


def wide_rows(rows, first, count):
    return jnp.concatenate([rows[first + n : first + n + 1, :] for n in range(count)], axis=1)


def fill_low_table(ref, columns):
    count = 16
    shape = (count, columns.shape[1])
    fine = parity_signs(iota(shape, 0), columns)
    coarse = parity_signs(iota(shape, 0), jnp.right_shift(columns, 4))
    for n in range(ref.shape[0] // count):
        ref[n * count : (n + 1) * count, :] = (fine * coarse[n : n + 1, :]).astype(BF16)


def fill_tables(kept, low_ref, high_ref):
    rows = wide_rows(kept, 0, kept.shape[0])
    fill_low_table(low_ref, rows)
    high_ref[...] = parity_signs(iota(high_ref.shape, 0), jnp.right_shift(rows, 8))


def split_moments(one_ref, two_ref):
    both = jnp.concatenate([one_ref[...], two_ref[...]], axis=1)
    half = both.shape[0] // 2
    return both[:half, :], both[half:, :]


def order_columns(half, kept):
    blocks = kept.shape[0]
    digits = jnp.concatenate([jnp.right_shift(kept, 7), jnp.bitwise_and(kept, LANES - 1)], axis=0)
    digits = digits.astype(F32).astype(BF16)
    source, target = iota((LANES, LANES), 0), iota((LANES, LANES), 1)
    same = jnp.logical_and(
        jnp.right_shift(source, 4) == jnp.bitwise_and(jnp.right_shift(target, 3), 7),
        jnp.bitwise_and(source, 7) == jnp.bitwise_and(target, 7),
    )
    source_half = jnp.bitwise_and(jnp.right_shift(source, 3), 1)
    pieces = []
    for wanted in (1 - half, half):
        moved = []
        for part in (0, 1):
            pick = jnp.logical_and(same, source_half == wanted)
            pick = jnp.logical_and(pick, jnp.right_shift(target, 6) == part)
            pick = jnp.where(pick, 1.0, 0.0).astype(BF16)
            moved.append(jnp.dot(digits, pick, preferred_element_type=F32))
        for pair in range(blocks // 2):
            even, odd = 2 * pair, 2 * pair + 1
            top = moved[0][even : even + 1, :] + moved[1][odd : odd + 1, :]
            low = (
                moved[0][blocks + even : blocks + even + 1, :]
                + moved[1][blocks + odd : blocks + odd + 1, :]
            )
            pieces.append(top * LANES + low)
    return jnp.concatenate(pieces, axis=1).astype(jnp.int32)


def project_half(scale, first, x_of, low_ref, high_ref, out_ref, acc_ref):
    rows, width = acc_ref.shape
    chunks = STEP // WIDE
    columns = slice(first, first + width)
    acc_ref[...] = jnp.zeros_like(acc_ref)

    def add(step, carry):
        x = x_of(step)
        stacked = jnp.concatenate([x[:, n * WIDE : (n + 1) * WIDE] for n in range(chunks)], axis=0)
        part = jnp.dot(stacked, low_ref[:, columns], preferred_element_type=F32)
        total = acc_ref[...]
        for n in range(chunks):
            sign = high_ref[pl.ds(step * chunks + n, 1), columns]
            total = total + part[n * rows : (n + 1) * rows, :] * sign
        acc_ref[...] = total
        return carry

    steps = high_ref.shape[0] // chunks
    lax.fori_loop(0, steps, add, 0, unroll=True)
    done = jnp.transpose(acc_ref[...] * scale).reshape((-1,) + out_ref.shape[1:])
    out_ref[: done.shape[0]] = done.astype(out_ref.dtype)


def project_other_kernel(
    scale, rep_ref, kept_hbm, bits_hbm, one_hbm, two_hbm, x_ref,
    low_ref, high_ref, signed_ref, out_ref,
    acc_ref, kept_ref, bits_ref, one_ref, two_ref, sems, small_sems,
):
    def fetch(step):
        lanes = pl.ds(pl.multiple_of(step * STEP, STEP), STEP)
        return pltpu.make_async_copy(x_ref.at[0, :, lanes], signed_ref.at[:, lanes], sems.at[step])

    pairs = ((kept_hbm, kept_ref), (bits_hbm, bits_ref), (one_hbm, one_ref), (two_hbm, two_ref))
    small = [
        pltpu.make_async_copy(far, near, small_sems.at[n]) for n, (far, near) in enumerate(pairs)
    ]
    for copy in small:
        copy.start()
    for step in range(signed_ref.shape[1] // STEP):
        fetch(step).start()
    for copy in small:
        copy.wait()
    half = jnp.bitwise_and(rep_ref[0], 1)
    columns = order_columns(half, kept_ref[...])
    fill_low_table(low_ref, columns)
    high_ref[...] = parity_signs(iota(high_ref.shape, 0), jnp.right_shift(columns, 8))
    upper, lower = split_moments(one_ref, two_ref)
    rest = jnp.where(half == 0, lower, upper)
    for n in range(PIECES):
        piece = rest.astype(BF16)
        out_ref[out_ref.shape[0] - PIECES + n] = piece
        rest = rest - piece.astype(F32)

    def x_of(step):
        fetch(step).wait()
        lanes = pl.ds(pl.multiple_of(step * STEP, STEP), STEP)
        signs = (1 - 2 * bits_ref[pl.ds(step * (STEP // LANES), STEP // LANES), :]).astype(F32)
        x = signed_ref[:, lanes] * wide_rows(signs, 0, STEP // LANES).astype(BF16)
        signed_ref[:, lanes] = x
        return x

    project_half(scale, 0, x_of, low_ref, high_ref, out_ref, acc_ref)


def project_own_kernel(scale, signed_ref, low_ref, high_ref, out_ref, acc_ref):
    def x_of(step):
        return signed_ref[:, pl.ds(pl.multiple_of(step * STEP, STEP), STEP)]

    project_half(scale, acc_ref.shape[1], x_of, low_ref, high_ref, out_ref, acc_ref)


def tables_kernel(
    rep_ref, kept_ref, one_ref, two_ref, other_ref, when_ref, low_ref, high_ref, moments_ref
):
    fill_tables(kept_ref[...], low_ref, high_ref)
    core = jnp.bitwise_and(rep_ref[0], 1)
    upper, lower = split_moments(one_ref, two_ref)
    same = jnp.where(core == 0, upper, lower)
    cross = jnp.zeros_like(same)
    for n in reversed(range(PIECES)):
        cross = cross + other_ref[other_ref.shape[0] - PIECES + n].astype(F32)
    moments_ref[0] = jnp.where(core == 0, same, cross)
    moments_ref[1] = jnp.where(core == 0, cross, same)


def turned_kernel(kept_ref, when_ref, turned_ref, high_ref, low_ref):
    fill_tables(kept_ref[...], low_ref, high_ref)
    turned_ref[...] = jnp.transpose(low_ref[...].astype(F32)).astype(BF16)


def compress_kernel(
    scale, panel_ref, y_ref, bits_ref, low_ref, high_ref, moments_ref, out_ref, part_ref
):
    sources, width, lanes = y_ref.shape
    line = sources // SIDE
    place = panel_ref[0] // line
    signs = bits_ref[pl.ds(pl.multiple_of(place * line, line), line), :]
    signs = (1 - 2 * signs).astype(F32)
    y = y_ref[...].astype(F32).reshape(SIDE, line, width, lanes) * signs[None, :, None, :]
    y = y.reshape(sources // 2, 2, width, lanes)
    y = jnp.concatenate([y[:, 0], y[:, 1]], axis=2).reshape(sources // 2 * width, 2 * lanes)
    part = jnp.dot(y.astype(BF16), low_ref[...], preferred_element_type=F32)
    part_ref[...] = part.reshape(part_ref.shape)
    total = jnp.zeros(part_ref.shape[2:], F32)
    for pair in range(line // 2):
        one = part_ref[0, pair]
        for other in range(1, SIDE):
            one = one + part_ref[other, pair]
        total = total + one * high_ref[pl.ds(place * (line // 2) + pair, 1), :]
    total = (total * scale).astype(BF16)
    pieces = [total[:, n : n + LANES] for n in range(0, total.shape[1], LANES)]
    first, second = moments_ref[0], moments_ref[1]
    middle = LANES // 2
    for lanes in (slice(0, middle), slice(middle, LANES)):
        rest = jnp.concatenate([first[:, lanes], second[:, lanes]], axis=1)
        for _ in range(PIECES):
            piece = rest.astype(BF16)
            pieces.append(piece)
            rest = rest - piece.astype(F32)
    for n, piece in enumerate(pieces):
        for peer in range(out_ref.shape[0]):
            out_ref[peer, n] = piece


def adam_kernel(
    scale, rep_ref, panel_ref, fix_ref, got_ref, bits_ref, turned_ref, high_ref,
    back_ref, sum_ref, lhs_ref,
):
    peers = got_ref.shape[0]
    line = back_ref.shape[1]
    place = panel_ref[0] // line
    mine = rep_ref[0] // (2 * SIDE) * SIDE + place
    first_fix, second_fix = fix_ref[0], fix_ref[1]
    tops, rests = [], []
    own = jnp.zeros(sum_ref.shape, F32)
    for n in range(peers):
        total = jnp.zeros(sum_ref.shape, F32)
        for peer in range(peers):
            total = total + got_ref[peer, n].astype(F32)
        own = jnp.where(mine == n, total, own)
        moments = []
        for index in range(2):
            moment = jnp.zeros(sum_ref.shape, F32)
            for piece in reversed(range(PIECES)):
                moment = moment + got_ref[n, peers + index * PIECES + piece].astype(F32)
            moments.append(moment)
        one, two = moments
        new_one = BETA_ONE * one + (1.0 - BETA_ONE) * total
        new_two = BETA_TWO * two + (1.0 - BETA_TWO) * total * total
        direction = new_one / first_fix / (jnp.sqrt(new_two / second_fix) + EPSILON)
        top = direction.astype(BF16).astype(F32)
        tops.append(top)
        rests.append(direction - top)
    sum_ref[...] = own
    both = jnp.concatenate([jnp.concatenate(tops, axis=1), jnp.concatenate(rests, axis=1)], axis=0)
    wides = lhs_ref.shape[0]
    for wide in range(wides):
        lhs_ref[wide] = (both * high_ref[pl.ds(place * wides + wide, 1), :]).astype(BF16)
    lhs = lhs_ref[...].reshape(wides * lhs_ref.shape[1], lhs_ref.shape[2])
    back = jnp.dot(lhs, turned_ref[...], preferred_element_type=F32)
    back = back.reshape(wides, 2, back.shape[0] // wides // 2, WIDE)
    back = back[:, 0] + back[:, 1]
    back = jnp.stack([back[:, :, :LANES], back[:, :, LANES:]], axis=1)
    back = back.reshape(2 * wides, back.shape[2], LANES)
    signs = bits_ref[pl.ds(pl.multiple_of(place * line, line), line), :]
    signs = (1 - 2 * signs).astype(F32) * scale
    back = (back * signs[:, None, :]).astype(BF16)
    for copy in range(SIDE):
        back_ref[copy] = back


def expand_kernel(
    scale, rep_ref, own_ref, other_ref, turned_ref, high_ref, bits_ref, weight_ref, out_ref,
    both_ref, back_ref, lhs_ref,
):
    step = pl.program_id(0)
    rows = weight_ref.shape[0]
    stride = out_ref.shape[1]
    chunks = stride // WIDE

    @pl.when(step == 0)
    def _():
        core = jnp.bitwise_and(rep_ref[0], 1)
        both_ref[:, pl.ds(core, 1)] = own_ref[...].astype(F32)[:, None]
        both_ref[:, pl.ds(1 - core, 1)] = other_ref[...].astype(F32)[:, None]
        columns = both_ref[...].reshape(back_ref.shape[1], rows)
        back_ref[...] = jnp.transpose(columns).astype(BF16)

    for chunk in range(chunks):
        sign = high_ref[pl.ds(step * chunks + chunk, 1), :].astype(BF16)
        lhs_ref[chunk * rows : (chunk + 1) * rows, :] = back_ref[...] * sign
    update = jnp.dot(lhs_ref[...], turned_ref[...], preferred_element_type=F32)
    tiles = stride // LANES
    signs = (1 - 2 * bits_ref[pl.ds(step * tiles, tiles), :]).astype(F32) * scale
    for chunk in range(chunks):
        lanes = pl.ds(pl.multiple_of(step * stride + chunk * WIDE, WIDE), WIDE)
        moved = update[chunk * rows : (chunk + 1) * rows, :] * wide_rows(signs, 2 * chunk, 2)
        moved = weight_ref[:, lanes].astype(F32) - moved
        out_ref[:, chunk * WIDE : (chunk + 1) * WIDE] = moved.astype(BF16)


def shaped(shape, dtype):
    return jax.ShapeDtypeStruct(shape, dtype)


SMEM = pl.BlockSpec(memory_space=pltpu.SMEM)
ROOM = pltpu.CompilerParams(vmem_limit_bytes=24 << 20)
VMEM = pl.BlockSpec(memory_space=pltpu.VMEM)


def cost(flops, moved):
    return pl.CostEstimate(flops=flops, bytes_accessed=moved, transcendentals=0)


def local(replica_grads, weight, moment_one, moment_two, sign_bits, kept_rows, step_count):
    reps, panels = lax.axis_size("rep"), lax.axis_size("fsdp")
    full_len, kept_len = sign_bits.shape[0], kept_rows.shape[0]
    rows = weight.shape[0]
    peers = reps // 2
    half_width = kept_len // panels // 2
    norm_scale = 1.0 / math.sqrt(kept_len)
    rep = lax.axis_index("rep").astype(jnp.int32).reshape(1)
    panel = lax.axis_index("fsdp").astype(jnp.int32).reshape(1)
    core = jnp.bitwise_and(rep[0], 1)
    kept = kept_rows.reshape(kept_len // LANES, LANES)
    bits = sign_bits.reshape(full_len // LANES, LANES)
    one_t, two_t = moment_one.T, moment_two.T
    wide_count = full_len // WIDE
    low_table, high_table = shaped((WIDE, kept_len), BF16), shaped((wide_count, kept_len), F32)
    everywhere = pl.BlockSpec(memory_space=pl.ANY)
    both = ("rep", "fsdp")
    swap = [(n, n ^ 1) for n in range(reps)]
    line, far = panels // SIDE, peers // SIDE
    near = range(SIDE)

    def device(y_hi, x, side, y_lo, z):
        return ((y_hi * SIDE + x) * 2 + side) * panels + y_lo * line + z

    planes = [
        [device(y_hi, x, side, y_lo, z) for x in near for z in range(line)]
        for y_hi in range(far) for side in range(2) for y_lo in near
    ]
    rings = [
        [device(y_hi, x, side, y_lo, z) for y_hi in range(far) for y_lo in near]
        for x in near for side in range(2) for z in range(line)
    ]

    def turn_over(cross):
        return [
            (device(y_hi, x, side, y_lo, z), device(y_hi, y_lo, side ^ cross, x, z))
            for y_hi in range(far) for x in near for side in range(2)
            for y_lo in near for z in range(line)
        ]

    def turn(when):
        return pl.pallas_call(
            turned_kernel,
            out_shape=(shaped((kept_len, WIDE), BF16), high_table),
            in_specs=[VMEM, everywhere],
            out_specs=(VMEM,) * 2,
            scratch_shapes=[pltpu.VMEM(low_table.shape, BF16)],
            compiler_params=ROOM,
            cost_estimate=cost(10 * LANES * kept_len, 8 * WIDE * kept_len),
        )(kept, when)

    def regroup(blocks, groups):
        return lax.all_to_all(blocks, both, 0, 0, axis_index_groups=groups, tiled=True)

    half_shape = (panels, half_width, rows)
    half_len = kept_len // 2
    in_hbm = [
        pltpu.with_memory_space_constraint(x, pltpu.HBM)
        for x in (kept, bits, one_t, two_t, replica_grads)
    ]
    col_low, col_high, signed, for_other = pl.pallas_call(
        functools.partial(project_other_kernel, norm_scale),
        out_shape=(
            low_table,
            high_table,
            shaped((rows, full_len), BF16),
            shaped((panels + PIECES, half_width, rows), BF16),
        ),
        in_specs=[SMEM] + [pl.BlockSpec(memory_space=pltpu.HBM)] * 5,
        out_specs=(VMEM,) * 4,
        scratch_shapes=[
            pltpu.VMEM((rows, half_len), F32),
            pltpu.VMEM(kept.shape, jnp.int32),
            pltpu.VMEM(bits.shape, jnp.int32),
            pltpu.VMEM(one_t.shape, F32),
            pltpu.VMEM(two_t.shape, F32),
            pltpu.SemaphoreType.DMA((full_len // STEP,)),
            pltpu.SemaphoreType.DMA((4,)),
        ],
        compiler_params=ROOM,
        cost_estimate=cost(2 * rows * full_len * half_len, 2 * rows * full_len),
    )(rep, *in_hbm)
    from_other = lax.ppermute(for_other, "rep", swap)
    mine = pl.pallas_call(
        functools.partial(project_own_kernel, norm_scale),
        out_shape=shaped(half_shape, F32),
        in_specs=[VMEM] * 3,
        out_specs=VMEM,
        scratch_shapes=[pltpu.VMEM((rows, half_len), F32)],
        compiler_params=ROOM,
        cost_estimate=cost(2 * rows * full_len * half_len, 2 * rows * full_len),
    )(signed, col_low, col_high)
    columns = (mine + from_other[:panels].astype(F32)).astype(BF16)
    low, high, moments = pl.pallas_call(
        tables_kernel,
        out_shape=(low_table, high_table, shaped((2, half_width, LANES), F32)),
        in_specs=[SMEM] + [VMEM] * 4 + [everywhere],
        out_specs=(VMEM,) * 3,
        compiler_params=ROOM,
        cost_estimate=cost(10 * LANES * kept_len, 8 * WIDE * kept_len),
    )(rep, kept, one_t, two_t, from_other, columns)
    moments = lax.ppermute(moments, both, turn_over(0))
    columns = regroup(columns, planes)

    message_shape = (peers, kept_len // LANES + 2 * PIECES, half_width, LANES)
    message = pl.pallas_call(
        functools.partial(compress_kernel, norm_scale),
        out_shape=shaped(message_shape, BF16),
        in_specs=[SMEM] + [VMEM] * 5,
        out_specs=VMEM,
        scratch_shapes=[pltpu.VMEM((SIDE, line // 2, half_width, kept_len), F32)],
        compiler_params=ROOM,
        cost_estimate=cost(2 * full_len * half_width * kept_len // panels, 2 * full_len * half_width),
    )(panel, columns, bits, low, high, moments)
    turned, high = turn(message)
    message = regroup(message, rings)

    steps_done = step_count.astype(F32)
    fixes = jnp.stack(
        [1.0 - jnp.power(F32(BETA_ONE), steps_done), 1.0 - jnp.power(F32(BETA_TWO), steps_done)]
    )
    back, own_sum = pl.pallas_call(
        functools.partial(adam_kernel, norm_scale),
        out_shape=(
            shaped((SIDE, line, half_width, rows), BF16),
            shaped((half_width, LANES), F32),
        ),
        in_specs=[SMEM] * 3 + [VMEM] * 4,
        out_specs=(VMEM,) * 2,
        scratch_shapes=[pltpu.VMEM((line // 2, 2 * half_width, kept_len), BF16)],
        compiler_params=ROOM,
        cost_estimate=cost(full_len * half_width * kept_len, 2 * full_len * half_width),
    )(rep, panel, fixes, message, bits, turned, high)
    turned, high = turn(back)
    same_sum = lax.ppermute(own_sum, both, turn_over(0))
    cross_sum = lax.ppermute(own_sum, both, turn_over(1))
    back = regroup(back.reshape(panels, half_width, rows), planes)
    other_back = lax.ppermute(back, "rep", swap)

    row_count = moment_one.shape[0]
    same_rows = jnp.where(core == 0, same_sum[:, :row_count], same_sum[:, row_count:])
    cross_rows = jnp.where(core == 0, cross_sum[:, :row_count], cross_sum[:, row_count:])
    compressed = jnp.where(
        core == 0,
        jnp.concatenate([same_rows, cross_rows], axis=0),
        jnp.concatenate([cross_rows, same_rows], axis=0),
    )
    new_one = (BETA_ONE * one_t + (1.0 - BETA_ONE) * compressed).T
    new_two = (BETA_TWO * two_t + (1.0 - BETA_TWO) * compressed * compressed).T

    new_weight = pl.pallas_call(
        functools.partial(expand_kernel, LEARN_RATE * norm_scale),
        grid=(full_len // LONG_STEP,),
        out_shape=shaped(weight.shape, BF16),
        in_specs=[SMEM] + [VMEM] * 6,
        out_specs=pl.BlockSpec((rows, LONG_STEP), lambda i: (0, i)),
        scratch_shapes=[
            pltpu.VMEM((panels, 2, half_width, rows), F32),
            pltpu.VMEM((rows, kept_len), BF16),
            pltpu.VMEM((rows * LONG_STEP // WIDE, kept_len), BF16),
        ],
        compiler_params=ROOM,
        cost_estimate=cost(2 * rows * full_len * kept_len, 4 * rows * full_len),
    )(rep, back, other_back, turned, high, bits, weight)
    return (new_weight, new_one, new_two)


def solution(mesh):
    in_specs = (
        P("rep", "fsdp", None),
        P("fsdp", None),
        P("rep", "fsdp"),
        P("rep", "fsdp"),
        P(),
        P(),
        P(),
    )
    out_specs = (P("fsdp", None), P("rep", "fsdp"), P("rep", "fsdp"))
    return jax.shard_map(local, mesh=mesh, in_specs=in_specs, out_specs=out_specs, check_vma=False)
```

```python
import functools
import math

import jax
import jax.numpy as jnp
from jax import lax
from jax.experimental import pallas as pl
from jax.experimental.pallas import tpu as pltpu
from jax.sharding import PartitionSpec as P

BETA_ONE = 0.9
BETA_TWO = 0.95
EPSILON = 1e-08
LEARN_RATE = 0.25
LANES = 128
WIDE = 256
STEP = 1024
SIDE = 4
PIECES = 2
F32 = jnp.float32
BF16 = jnp.bfloat16


def parity_signs(left, right):
    both = jnp.bitwise_and(left, right)
    for shift in (4, 2, 1):
        both = jnp.bitwise_xor(both, jnp.right_shift(both, shift))
    return (1 - 2 * jnp.bitwise_and(both, 1)).astype(F32)


def iota(shape, dim):
    return lax.broadcasted_iota(jnp.int32, shape, dim)


def wide_rows(rows, first, count):
    return jnp.concatenate([rows[first + n : first + n + 1, :] for n in range(count)], axis=1)


def fill_low_table(ref, columns):
    count = 16
    shape = (count, columns.shape[1])
    fine = parity_signs(iota(shape, 0), columns)
    coarse = parity_signs(iota(shape, 0), jnp.right_shift(columns, 4))
    for n in range(ref.shape[0] // count):
        ref[n * count : (n + 1) * count, :] = (fine * coarse[n : n + 1, :]).astype(BF16)


def fill_tables(kept, low_ref, high_ref):
    rows = wide_rows(kept, 0, kept.shape[0])
    fill_low_table(low_ref, rows)
    high_ref[...] = parity_signs(iota(high_ref.shape, 0), jnp.right_shift(rows, 8))


def split_moments(one_ref, two_ref):
    both = jnp.concatenate([one_ref[...], two_ref[...]], axis=1)
    half = both.shape[0] // 2
    return both[:half, :], both[half:, :]


def order_columns(half, kept):
    blocks = kept.shape[0]
    digits = jnp.concatenate([jnp.right_shift(kept, 7), jnp.bitwise_and(kept, LANES - 1)], axis=0)
    digits = digits.astype(F32).astype(BF16)
    source, target = iota((LANES, LANES), 0), iota((LANES, LANES), 1)
    same = jnp.logical_and(
        jnp.right_shift(source, 4) == jnp.bitwise_and(jnp.right_shift(target, 3), 7),
        jnp.bitwise_and(source, 7) == jnp.bitwise_and(target, 7),
    )
    source_half = jnp.bitwise_and(jnp.right_shift(source, 3), 1)
    pieces = []
    for wanted in (1 - half, half):
        moved = []
        for part in (0, 1):
            pick = jnp.logical_and(same, source_half == wanted)
            pick = jnp.logical_and(pick, jnp.right_shift(target, 6) == part)
            pick = jnp.where(pick, 1.0, 0.0).astype(BF16)
            moved.append(jnp.dot(digits, pick, preferred_element_type=F32))
        for pair in range(blocks // 2):
            even, odd = 2 * pair, 2 * pair + 1
            top = moved[0][even : even + 1, :] + moved[1][odd : odd + 1, :]
            low = (
                moved[0][blocks + even : blocks + even + 1, :]
                + moved[1][blocks + odd : blocks + odd + 1, :]
            )
            pieces.append(top * LANES + low)
    return jnp.concatenate(pieces, axis=1).astype(jnp.int32)


def project_half(scale, first, x_of, low_ref, high_ref, out_ref, acc_ref):
    rows, width = acc_ref.shape
    chunks = STEP // WIDE
    columns = slice(first, first + width)
    acc_ref[...] = jnp.zeros_like(acc_ref)

    def add(step, carry):
        x = x_of(step)
        stacked = jnp.concatenate([x[:, n * WIDE : (n + 1) * WIDE] for n in range(chunks)], axis=0)
        part = jnp.dot(stacked, low_ref[:, columns], preferred_element_type=F32)
        total = acc_ref[...]
        for n in range(chunks):
            sign = high_ref[pl.ds(step * chunks + n, 1), columns]
            total = total + part[n * rows : (n + 1) * rows, :] * sign
        acc_ref[...] = total
        return carry

    steps = high_ref.shape[0] // chunks
    lax.fori_loop(0, steps, add, 0, unroll=True)
    done = jnp.transpose(acc_ref[...] * scale).reshape((-1,) + out_ref.shape[1:])
    out_ref[: done.shape[0]] = done.astype(out_ref.dtype)


def project_other_kernel(
    scale, rep_ref, kept_hbm, bits_hbm, one_hbm, two_hbm, x_ref,
    low_ref, high_ref, signed_ref, out_ref,
    acc_ref, kept_ref, bits_ref, one_ref, two_ref, sems, small_sems,
):
    def fetch(step):
        lanes = pl.ds(pl.multiple_of(step * STEP, STEP), STEP)
        return pltpu.make_async_copy(x_ref.at[0, :, lanes], signed_ref.at[:, lanes], sems.at[step])

    pairs = ((kept_hbm, kept_ref), (bits_hbm, bits_ref), (one_hbm, one_ref), (two_hbm, two_ref))
    small = [
        pltpu.make_async_copy(far, near, small_sems.at[n]) for n, (far, near) in enumerate(pairs)
    ]
    for copy in small:
        copy.start()
    for step in range(signed_ref.shape[1] // STEP):
        fetch(step).start()
    for copy in small:
        copy.wait()
    half = jnp.bitwise_and(rep_ref[0], 1)
    columns = order_columns(half, kept_ref[...])
    fill_low_table(low_ref, columns)
    high_ref[...] = parity_signs(iota(high_ref.shape, 0), jnp.right_shift(columns, 8))
    upper, lower = split_moments(one_ref, two_ref)
    rest = jnp.where(half == 0, lower, upper)
    for n in range(PIECES):
        piece = rest.astype(BF16)
        out_ref[out_ref.shape[0] - PIECES + n] = piece
        rest = rest - piece.astype(F32)

    def x_of(step):
        fetch(step).wait()
        lanes = pl.ds(pl.multiple_of(step * STEP, STEP), STEP)
        signs = (1 - 2 * bits_ref[pl.ds(step * (STEP // LANES), STEP // LANES), :]).astype(F32)
        x = signed_ref[:, lanes] * wide_rows(signs, 0, STEP // LANES).astype(BF16)
        signed_ref[:, lanes] = x
        return x

    project_half(scale, 0, x_of, low_ref, high_ref, out_ref, acc_ref)


def project_own_kernel(scale, signed_ref, low_ref, high_ref, out_ref, acc_ref):
    def x_of(step):
        return signed_ref[:, pl.ds(pl.multiple_of(step * STEP, STEP), STEP)]

    project_half(scale, acc_ref.shape[1], x_of, low_ref, high_ref, out_ref, acc_ref)


def tables_kernel(
    rep_ref, kept_ref, one_ref, two_ref, other_ref, when_ref, low_ref, high_ref, moments_ref
):
    fill_tables(kept_ref[...], low_ref, high_ref)
    core = jnp.bitwise_and(rep_ref[0], 1)
    upper, lower = split_moments(one_ref, two_ref)
    same = jnp.where(core == 0, upper, lower)
    cross = jnp.zeros_like(same)
    for n in reversed(range(PIECES)):
        cross = cross + other_ref[other_ref.shape[0] - PIECES + n].astype(F32)
    moments_ref[0] = jnp.where(core == 0, same, cross)
    moments_ref[1] = jnp.where(core == 0, cross, same)


def turned_kernel(kept_ref, when_ref, turned_ref, high_ref, low_ref):
    fill_tables(kept_ref[...], low_ref, high_ref)
    turned_ref[...] = jnp.transpose(low_ref[...].astype(F32)).astype(BF16)


def turned_and_sums_kernel(
    rep_ref, kept_ref, own_ref, other_ref, when_ref, turned_ref, high_ref, sums_ref, low_ref
):
    turned_kernel(kept_ref, when_ref, turned_ref, high_ref, low_ref)
    core = jnp.bitwise_and(rep_ref[0], 1)
    own, other = own_ref[...], other_ref[...]
    middle = LANES // 2
    sums_ref[...] = jnp.where(
        core == 0,
        jnp.concatenate([own[:, :middle], other[:, :middle]], axis=1),
        jnp.concatenate([other[:, middle:], own[:, middle:]], axis=1),
    )


def compress_kernel(
    scale, panel_ref, y_ref, bits_ref, low_ref, high_ref, moments_ref, out_ref, part_ref
):
    sources, width, lanes = y_ref.shape
    line = sources // SIDE
    place = panel_ref[0] // line
    signs = bits_ref[pl.ds(pl.multiple_of(place * line, line), line), :]
    signs = (1 - 2 * signs).astype(F32)
    y = y_ref[...].astype(F32).reshape(SIDE, line, width, lanes) * signs[None, :, None, :]
    y = y.reshape(sources // 2, 2, width, lanes)
    y = jnp.concatenate([y[:, 0], y[:, 1]], axis=2).reshape(sources // 2 * width, 2 * lanes)
    part = jnp.dot(y.astype(BF16), low_ref[...], preferred_element_type=F32)
    part_ref[...] = part.reshape(part_ref.shape)
    total = jnp.zeros(part_ref.shape[2:], F32)
    for pair in range(line // 2):
        one = part_ref[0, pair]
        for other in range(1, SIDE):
            one = one + part_ref[other, pair]
        total = total + one * high_ref[pl.ds(place * (line // 2) + pair, 1), :]
    total = (total * scale).astype(BF16)
    pieces = [total[:, n : n + LANES] for n in range(0, total.shape[1], LANES)]
    first, second = moments_ref[0], moments_ref[1]
    middle = LANES // 2
    for lanes in (slice(0, middle), slice(middle, LANES)):
        rest = jnp.concatenate([first[:, lanes], second[:, lanes]], axis=1)
        for _ in range(PIECES):
            piece = rest.astype(BF16)
            pieces.append(piece)
            rest = rest - piece.astype(F32)
    for n, piece in enumerate(pieces):
        for peer in range(out_ref.shape[0]):
            out_ref[peer, n] = piece


def adam_kernel(
    scale, rep_ref, panel_ref, fix_ref, got_ref, bits_ref, turned_ref, high_ref,
    back_ref, sum_ref, lhs_ref,
):
    peers = got_ref.shape[0]
    line = back_ref.shape[1]
    place = panel_ref[0] // line
    mine = rep_ref[0] // (2 * SIDE) * SIDE + place
    first_fix, second_fix = fix_ref[0], fix_ref[1]
    tops, rests = [], []
    own = jnp.zeros(sum_ref.shape, F32)
    for n in range(peers):
        total = jnp.zeros(sum_ref.shape, F32)
        for peer in range(peers):
            total = total + got_ref[peer, n].astype(F32)
        own = jnp.where(mine == n, total, own)
        moments = []
        for index in range(2):
            moment = jnp.zeros(sum_ref.shape, F32)
            for piece in reversed(range(PIECES)):
                moment = moment + got_ref[n, peers + index * PIECES + piece].astype(F32)
            moments.append(moment)
        one, two = moments
        new_one = BETA_ONE * one + (1.0 - BETA_ONE) * total
        new_two = BETA_TWO * two + (1.0 - BETA_TWO) * total * total
        direction = new_one / first_fix / (jnp.sqrt(new_two / second_fix) + EPSILON)
        top = direction.astype(BF16).astype(F32)
        tops.append(top)
        rests.append(direction - top)
    sum_ref[...] = own
    both = jnp.concatenate([jnp.concatenate(tops, axis=1), jnp.concatenate(rests, axis=1)], axis=0)
    wides = lhs_ref.shape[0]
    for wide in range(wides):
        lhs_ref[wide] = (both * high_ref[pl.ds(place * wides + wide, 1), :]).astype(BF16)
    lhs = lhs_ref[...].reshape(wides * lhs_ref.shape[1], lhs_ref.shape[2])
    back = jnp.dot(lhs, turned_ref[...], preferred_element_type=F32)
    back = back.reshape(wides, 2, back.shape[0] // wides // 2, WIDE)
    back = back[:, 0] + back[:, 1]
    back = jnp.stack([back[:, :, :LANES], back[:, :, LANES:]], axis=1)
    back = back.reshape(2 * wides, back.shape[2], LANES)
    signs = bits_ref[pl.ds(pl.multiple_of(place * line, line), line), :]
    signs = (1 - 2 * signs).astype(F32) * scale
    back = (back * signs[:, None, :]).astype(BF16)
    for copy in range(SIDE):
        back_ref[copy] = back


def expand_kernel(
    scale, rep_ref, own_ref, other_ref, turned_ref, high_ref, bits_ref, weight_ref, out_hbm,
    both_ref, lhs_ref, out_ref, sems,
):
    rows = weight_ref.shape[0]
    chunks = STEP // WIDE
    tiles = STEP // LANES
    core = jnp.bitwise_and(rep_ref[0], 1)
    both_ref[:, pl.ds(core, 1)] = own_ref[...].astype(F32)[:, None]
    both_ref[:, pl.ds(1 - core, 1)] = other_ref[...].astype(F32)[:, None]
    back = jnp.transpose(both_ref[...].reshape(turned_ref.shape[0], rows)).astype(BF16)
    steps = weight_ref.shape[1] // STEP

    def store(step):
        lanes = slice(step * STEP, (step + 1) * STEP)
        return pltpu.make_async_copy(out_ref.at[:, lanes], out_hbm.at[:, lanes], sems.at[step])

    for step in range(steps):
        slot = step % 2
        for chunk in range(chunks):
            wide = step * chunks + chunk
            sign = high_ref[wide : wide + 1, :].astype(BF16)
            lhs_ref[slot, chunk * rows : (chunk + 1) * rows, :] = back * sign
        update = jnp.dot(lhs_ref[slot], turned_ref[...], preferred_element_type=F32)
        signs = (1 - 2 * bits_ref[step * tiles : (step + 1) * tiles, :]).astype(F32) * scale
        for chunk in range(chunks):
            first = step * STEP + chunk * WIDE
            lanes = slice(first, first + WIDE)
            moved = update[chunk * rows : (chunk + 1) * rows, :] * wide_rows(signs, 2 * chunk, 2)
            out_ref[:, lanes] = (weight_ref[:, lanes].astype(F32) - moved).astype(BF16)
        store(step).start()
    for step in range(steps):
        store(step).wait()


def shaped(shape, dtype):
    return jax.ShapeDtypeStruct(shape, dtype)


SMEM = pl.BlockSpec(memory_space=pltpu.SMEM)
ROOM = pltpu.CompilerParams(vmem_limit_bytes=24 << 20)
VMEM = pl.BlockSpec(memory_space=pltpu.VMEM)


def cost(flops, moved):
    return pl.CostEstimate(flops=flops, bytes_accessed=moved, transcendentals=0)


def local(replica_grads, weight, moment_one, moment_two, sign_bits, kept_rows, step_count):
    reps, panels = lax.axis_size("rep"), lax.axis_size("fsdp")
    full_len, kept_len = sign_bits.shape[0], kept_rows.shape[0]
    rows = weight.shape[0]
    peers = reps // 2
    half_width = kept_len // panels // 2
    norm_scale = 1.0 / math.sqrt(kept_len)
    rep = lax.axis_index("rep").astype(jnp.int32).reshape(1)
    panel = lax.axis_index("fsdp").astype(jnp.int32).reshape(1)
    kept = kept_rows.reshape(kept_len // LANES, LANES)
    bits = sign_bits.reshape(full_len // LANES, LANES)
    one_t, two_t = moment_one.T, moment_two.T
    wide_count = full_len // WIDE
    low_table, high_table = shaped((WIDE, kept_len), BF16), shaped((wide_count, kept_len), F32)
    everywhere = pl.BlockSpec(memory_space=pl.ANY)
    both = ("rep", "fsdp")
    swap = [(n, n ^ 1) for n in range(reps)]
    line, far = panels // SIDE, peers // SIDE
    near = range(SIDE)

    def device(y_hi, x, side, y_lo, z):
        return ((y_hi * SIDE + x) * 2 + side) * panels + y_lo * line + z

    planes = [
        [device(y_hi, x, side, y_lo, z) for x in near for z in range(line)]
        for y_hi in range(far) for side in range(2) for y_lo in near
    ]
    rings = [
        [device(y_hi, x, side, y_lo, z) for y_hi in range(far) for y_lo in near]
        for x in near for side in range(2) for z in range(line)
    ]

    def turn_over():
        return [
            (device(y_hi, x, side, y_lo, z), device(y_hi, y_lo, side, x, z))
            for y_hi in range(far) for x in near for side in range(2)
            for y_lo in near for z in range(line)
        ]

    def turn(when):
        return pl.pallas_call(
            turned_kernel,
            out_shape=(shaped((kept_len, WIDE), BF16), high_table),
            in_specs=[VMEM, everywhere],
            out_specs=(VMEM,) * 2,
            scratch_shapes=[pltpu.VMEM(low_table.shape, BF16)],
            compiler_params=ROOM,
            cost_estimate=cost(10 * LANES * kept_len, 8 * WIDE * kept_len),
        )(kept, when)

    def regroup(blocks, groups):
        return lax.all_to_all(blocks, both, 0, 0, axis_index_groups=groups, tiled=True)

    half_shape = (panels, half_width, rows)
    half_len = kept_len // 2
    half_moments = shaped((half_width, LANES), F32)
    in_hbm = [
        pltpu.with_memory_space_constraint(x, pltpu.HBM)
        for x in (kept, bits, one_t, two_t, replica_grads)
    ]
    col_low, col_high, signed, for_other = pl.pallas_call(
        functools.partial(project_other_kernel, norm_scale),
        out_shape=(
            low_table,
            high_table,
            shaped((rows, full_len), BF16),
            shaped((panels + PIECES, half_width, rows), BF16),
        ),
        in_specs=[SMEM] + [pl.BlockSpec(memory_space=pltpu.HBM)] * 5,
        out_specs=(VMEM,) * 4,
        scratch_shapes=[
            pltpu.VMEM((rows, half_len), F32),
            pltpu.VMEM(kept.shape, jnp.int32),
            pltpu.VMEM(bits.shape, jnp.int32),
            pltpu.VMEM(one_t.shape, F32),
            pltpu.VMEM(two_t.shape, F32),
            pltpu.SemaphoreType.DMA((full_len // STEP,)),
            pltpu.SemaphoreType.DMA((4,)),
        ],
        compiler_params=ROOM,
        cost_estimate=cost(2 * rows * full_len * half_len, 2 * rows * full_len),
    )(rep, *in_hbm)
    from_other = lax.ppermute(for_other, "rep", swap)
    mine = pl.pallas_call(
        functools.partial(project_own_kernel, norm_scale),
        out_shape=shaped(half_shape, F32),
        in_specs=[VMEM] * 3,
        out_specs=VMEM,
        scratch_shapes=[pltpu.VMEM((rows, half_len), F32)],
        compiler_params=ROOM,
        cost_estimate=cost(2 * rows * full_len * half_len, 2 * rows * full_len),
    )(signed, col_low, col_high)
    columns = (mine + from_other[:panels].astype(F32)).astype(BF16)
    low, high, moments = pl.pallas_call(
        tables_kernel,
        out_shape=(low_table, high_table, shaped((2, half_width, LANES), F32)),
        in_specs=[SMEM] + [VMEM] * 4 + [everywhere],
        out_specs=(VMEM,) * 3,
        compiler_params=ROOM,
        cost_estimate=cost(10 * LANES * kept_len, 8 * WIDE * kept_len),
    )(rep, kept, one_t, two_t, from_other, columns)
    moments = lax.ppermute(moments, both, turn_over())
    columns = regroup(columns, planes)

    message_shape = (peers, kept_len // LANES + 2 * PIECES, half_width, LANES)
    message = pl.pallas_call(
        functools.partial(compress_kernel, norm_scale),
        out_shape=shaped(message_shape, BF16),
        in_specs=[SMEM] + [VMEM] * 5,
        out_specs=VMEM,
        scratch_shapes=[pltpu.VMEM((SIDE, line // 2, half_width, kept_len), F32)],
        compiler_params=ROOM,
        cost_estimate=cost(2 * full_len * half_width * kept_len // panels, 2 * full_len * half_width),
    )(panel, columns, bits, low, high, moments)
    turned, high = turn(message)
    message = regroup(message, rings)

    steps_done = step_count.astype(F32)
    fixes = jnp.stack(
        [1.0 - jnp.power(F32(BETA_ONE), steps_done), 1.0 - jnp.power(F32(BETA_TWO), steps_done)]
    )
    back, own_sum = pl.pallas_call(
        functools.partial(adam_kernel, norm_scale),
        out_shape=(
            shaped((SIDE, line, half_width, rows), BF16),
            shaped((half_width, LANES), F32),
        ),
        in_specs=[SMEM] * 3 + [VMEM] * 4,
        out_specs=(VMEM,) * 2,
        scratch_shapes=[pltpu.VMEM((line // 2, 2 * half_width, kept_len), BF16)],
        compiler_params=ROOM,
        cost_estimate=cost(full_len * half_width * kept_len, 2 * full_len * half_width),
    )(rep, panel, fixes, message, bits, turned, high)
    other_sum = lax.ppermute(own_sum, "rep", swap)
    turned, high, sums = pl.pallas_call(
        turned_and_sums_kernel,
        out_shape=(shaped((kept_len, WIDE), BF16), high_table, half_moments),
        in_specs=[SMEM] + [VMEM] * 3 + [everywhere],
        out_specs=(VMEM,) * 3,
        scratch_shapes=[pltpu.VMEM(low_table.shape, BF16)],
        compiler_params=ROOM,
        cost_estimate=cost(10 * LANES * kept_len, 8 * WIDE * kept_len),
    )(rep, kept, own_sum, other_sum, back)
    sums = lax.ppermute(sums, both, turn_over())
    back = regroup(back.reshape(panels, half_width, rows), planes)
    other_back = lax.ppermute(back, "rep", swap)

    row_count = moment_one.shape[0]
    compressed = jnp.concatenate([sums[:, :row_count], sums[:, row_count:]], axis=0)
    new_one = (BETA_ONE * one_t + (1.0 - BETA_ONE) * compressed).T
    new_two = (BETA_TWO * two_t + (1.0 - BETA_TWO) * compressed * compressed).T

    new_weight = pl.pallas_call(
        functools.partial(expand_kernel, LEARN_RATE * norm_scale),
        out_shape=shaped(weight.shape, BF16),
        in_specs=[SMEM] + [VMEM] * 6,
        out_specs=pl.BlockSpec(memory_space=pltpu.HBM),
        scratch_shapes=[
            pltpu.VMEM((panels, 2, half_width, rows), F32),
            pltpu.VMEM((2, rows * STEP // WIDE, kept_len), BF16),
            pltpu.VMEM(weight.shape, BF16),
            pltpu.SemaphoreType.DMA((full_len // STEP,)),
        ],
        compiler_params=ROOM,
        cost_estimate=cost(2 * rows * full_len * kept_len, 4 * rows * full_len),
    )(rep, back, other_back, turned, high, bits, weight)
    return (new_weight, new_one, new_two)


def solution(mesh):
    in_specs = (
        P("rep", "fsdp", None),
        P("fsdp", None),
        P("rep", "fsdp"),
        P("rep", "fsdp"),
        P(),
        P(),
        P(),
    )
    out_specs = (P("fsdp", None), P("rep", "fsdp"), P("rep", "fsdp"))
    return jax.shard_map(local, mesh=mesh, in_specs=in_specs, out_specs=out_specs, check_vma=False)
```
